32 devices in a mesh: rep: 2 (over y), head: 4 (over z), ctx: 4 (over x, core).
Axes of the slice: x: 2, y: 2, z: 4, core: 2. Of those that a mesh axis runs over, the one named last changes fastest.
Arguments:
- queries: bfloat16 [8, 512, 8192], P(('rep', 'ctx'), 'head'), parts along dimension 0, may hold values from -6 to 6
- keys: bfloat16 [8, 512, 8192], P(('rep', 'ctx'), 'head'), parts along dimension 0, may hold values from -6 to 6
- values: bfloat16 [8, 512, 8192], P(('rep', 'ctx'), 'head'), parts along dimension 0, may hold values from -6 to 6
- gain: float32 [8192], replicated, may hold values from 0.5 to 1.5
Outputs:
- normed: bfloat16 [8, 512, 8192], P(('rep', 'ctx'), 'head'), parts along dimension 0
The draws below stay inside these ranges and needn't reach their ends.
There are 2 independent parts, one for each index of `rep`. The reference program is written for one: setup_inputs(seed, part) draws one part's arguments, and reference() takes and returns one part's arrays. A program takes and returns all parts, laid end to end along the dimension named above; an argument that names none is the same for every part. Nothing has to cross between parts.
All inputs are finite; a program needn't handle non-finite values.
Results may differ from the reference program's by a relative error of at most 0.0059.
Values may be sent and summed in bfloat16 or wider, within the bound.
No kernel may reach another device: no remote copies, remote signals or barrier semaphores. Data moves between devices by JAX's collectives and lax.ppermute only.
A program may use at most 128 MiB of HBM per device.

```python
import jax
import jax.numpy as jnp
from jax import lax

H = 64
DH = 128
WIDE = 8192
SPAN = 512
BLK = 128
CHAINS = 4


def block_scale(stream_key, shape, pieces, smallest, largest):
    factor_of = 1.0
    for axis_at, shards_of in pieces:
        steps = jax.random.uniform(jax.random.fold_in(jax.random.fold_in(stream_key, 6), axis_at), (shards_of,), jnp.float32, smallest / len(pieces), largest / len(pieces))
        factor_of = factor_of * jnp.repeat(jnp.exp(steps), shape[axis_at] // shards_of).reshape((-1,) + (1,) * (len(shape) - 1 - axis_at))
    return factor_of


def centred(stream_key, dims, scale, limit, shards=(), kind=jnp.bfloat16):
    factor_of = block_scale(stream_key, dims, shards, -0.22, 0.18) if shards else 1.0
    array = jax.random.normal(stream_key, dims, jnp.float32) * scale * factor_of
    return jnp.minimum(jnp.maximum(array, -limit), limit).astype(kind)


def setup_inputs(seed: int = 0, part: int = 0) -> dict:
    seeds = jax.random.split(jax.random.key(seed), 5)
    own_keys = jax.random.split(jax.random.fold_in(seeds[4], part), 5)
    queries = centred(own_keys[0], (CHAINS, SPAN, WIDE), 1.0, 6.0, ((0, 4), (1, 4)))
    keys = centred(own_keys[1], (CHAINS, SPAN, WIDE), 1.0, 6.0, ((0, 4), (1, 4)))
    values = centred(own_keys[2], (CHAINS, SPAN, WIDE), 1.0, 6.0, ((0, 4), (1, 4)))
    gain = jnp.clip(1.0 + 0.1 * jax.random.normal(seeds[3], (WIDE,), jnp.float32), 0.5, 1.5)
    return dict(queries=queries, keys=keys, values=values, gain=gain)


def one_head(qa_head, ka_head, values_head):
    blocks = qa_head.shape[0] // BLK
    qb = qa_head.reshape(blocks, BLK, DH)
    kb = ka_head.reshape(blocks, BLK, DH)
    vb = values_head.reshape(blocks, BLK, DH)
    causal = jnp.arange(BLK)[:, None] >= jnp.arange(BLK)[None, :]

    def step(carry, item):
        query_blk, key_blk, value_blk = item
        state = carry.astype(jnp.bfloat16)
        scores = jnp.dot(query_blk, key_blk.T, preferred_element_type=jnp.float32)
        scores = jnp.where(causal, scores, jnp.float32(0.0)).astype(jnp.bfloat16)
        local_part = jnp.dot(scores, value_blk, preferred_element_type=jnp.float32)
        carried = jnp.dot(query_blk, state, preferred_element_type=jnp.float32)
        attn = (local_part + carried).astype(jnp.bfloat16)
        carry = carry + jnp.dot(key_blk.T, value_blk, preferred_element_type=jnp.float32)
        return (carry, attn)
    init = jnp.zeros((DH, DH), jnp.float32)
    final_state, outputs = lax.scan(step, init, (qb, kb, vb))
    return outputs.reshape(blocks * BLK, DH)

def reference(queries, keys, values, gain):
    total = queries.shape[0] * queries.shape[1]
    width = H * DH
    q_rows = queries.reshape(total, width)
    k_rows = keys.reshape(total, width)
    v_rows = values.reshape(total, width)
    qa = jax.nn.silu(q_rows.astype(jnp.float32)).astype(jnp.bfloat16)
    ka = jax.nn.silu(k_rows.astype(jnp.float32)).astype(jnp.bfloat16)
    qh = qa.reshape(total, H, DH).transpose(1, 0, 2)
    kh = ka.reshape(total, H, DH).transpose(1, 0, 2)
    vh = v_rows.reshape(total, H, DH).transpose(1, 0, 2)
    attn = lax.map(lambda item: one_head(item[0], item[1], item[2]), (qh, kh, vh))
    attn = attn.transpose(1, 0, 2).reshape(total, width)
    wide = attn.astype(jnp.float32)
    mean_sq = lax.optimization_barrier(jnp.mean(wide * wide, axis=1, keepdims=True))
    normed = wide * lax.rsqrt(mean_sq + 1e-06) * gain[None, :]
    return normed.astype(jnp.bfloat16).reshape(queries.shape)
```

```python
import functools

import jax
import jax.numpy as jnp
from jax import lax
from jax.experimental import pallas as pl
from jax.experimental.pallas import tpu as pltpu
from jax.sharding import PartitionSpec as P

DH = 128
F32 = jnp.float32
BF16 = jnp.bfloat16


def silu(x):
    x = x.astype(F32)
    return (x / (1.0 + jnp.exp(-x))).astype(BF16)


def kv_kernel(heads, k_ref, v_ref, c_ref):
    for h in range(heads):
        cols = slice(h * DH, (h + 1) * DH)
        ka = silu(k_ref[:, cols])
        c_ref[h] = lax.dot_general(
            ka, v_ref[:, cols], (((0,), (0,)), ((), ())), preferred_element_type=F32
        ).astype(BF16)


def kv_states(k_rows, v_rows, first, count, step):
    rows = k_rows.shape[0]
    base = first // step
    block = pl.BlockSpec((rows, step * DH), lambda i: (0, base + i))
    return pl.pallas_call(
        functools.partial(kv_kernel, step),
        grid=(count // step,),
        in_specs=[block, block],
        out_specs=pl.BlockSpec((step, DH, DH), lambda i: (i, 0, 0)),
        out_shape=jax.ShapeDtypeStruct((count, DH, DH), BF16),
        cost_estimate=pl.CostEstimate(
            flops=2 * count * rows * DH * DH,
            bytes_accessed=2 * count * DH * (2 * rows + DH),
            transcendentals=count * DH * rows,
        ),
        name="kv_states",
    )(k_rows, v_rows)


def local_kernel(heads, q_ref, k_ref, v_ref, qa_ref, part_ref):
    rows = q_ref.shape[0]
    causal = lax.broadcasted_iota(jnp.int32, (rows, rows), 0) >= lax.broadcasted_iota(
        jnp.int32, (rows, rows), 1
    )
    for h in range(heads):
        cols = slice(h * DH, (h + 1) * DH)
        qa = silu(q_ref[:, cols])
        ka = silu(k_ref[:, cols])
        scores = lax.dot_general(
            qa, ka, (((1,), (1,)), ((), ())), preferred_element_type=F32
        )
        scores = jnp.where(causal, scores, 0.0).astype(BF16)
        part_ref[:, cols] = jnp.dot(
            scores, v_ref[:, cols], preferred_element_type=F32
        )
        qa_ref[:, cols] = qa


def local_parts(q_rows, k_rows, v_rows, first, count, step):
    rows = q_rows.shape[0]
    base = first // step
    block = pl.BlockSpec((rows, step * DH), lambda i: (0, base + i))
    out = pl.BlockSpec((rows, step * DH), lambda i: (0, i))
    return pl.pallas_call(
        functools.partial(local_kernel, step),
        grid=(count // step,),
        in_specs=[block, block, block],
        out_specs=[out, out],
        out_shape=[
            jax.ShapeDtypeStruct((rows, count * DH), BF16),
            jax.ShapeDtypeStruct((rows, count * DH), F32),
        ],
        cost_estimate=pl.CostEstimate(
            flops=4 * count * rows * rows * DH,
            bytes_accessed=12 * count * DH * rows,
            transcendentals=2 * count * DH * rows,
        ),
        name="local_parts",
    )(q_rows, k_rows, v_rows)


def attend_kernel(heads, qa_ref, part_ref, in_ref, out_ref, f_ref, attn_ref, sq_ref):
    total = None
    for h in range(heads):
        cols = slice(h * DH, (h + 1) * DH)
        state = (
            in_ref[h].astype(F32) + out_ref[h].astype(F32) + f_ref[h].astype(F32)
        ).astype(BF16)
        carried = jnp.dot(qa_ref[:, cols], state, preferred_element_type=F32)
        attn = (part_ref[:, cols] + carried).astype(BF16)
        attn_ref[:, cols] = attn
        wide = attn.astype(F32)
        total = wide * wide if total is None else total + wide * wide
    sq_ref[...] = total


def attend(qa, part, inward, outward, early):
    rows, width = qa.shape
    heads = width // DH
    return pl.pallas_call(
        functools.partial(attend_kernel, heads),
        out_shape=[
            jax.ShapeDtypeStruct((rows, width), BF16),
            jax.ShapeDtypeStruct((rows, DH), F32),
        ],
        cost_estimate=pl.CostEstimate(
            flops=2 * heads * rows * DH * DH,
            bytes_accessed=8 * rows * width + 6 * heads * DH * DH,
            transcendentals=0,
        ),
        name="attend",
    )(qa, part, inward, outward, early)


def norm_kernel(sizes, *refs):
    n = len(sizes)
    attn_refs, sq_refs, gain_ref, out_ref = refs[:n], refs[n : 2 * n], refs[2 * n], refs[2 * n + 1]
    total = sq_refs[0][...]
    for ref in sq_refs[1:]:
        total = total + ref[...]
    mean_sq = jnp.sum(total, axis=1, keepdims=True) / sum(sizes)
    scale = lax.rsqrt(mean_sq + 1e-06)
    at = 0
    for ref, size in zip(attn_refs, sizes):
        for c in range(0, size, 512):
            wide = min(512, size - c)
            out_ref[0, :, at + c : at + c + wide] = (
                ref[:, c : c + wide].astype(F32) * scale * gain_ref[:, at + c : at + c + wide]
            ).astype(BF16)
        at += size


def row_norm(attns, squares, gain):
    rows = attns[0].shape[0]
    sizes = [a.shape[1] for a in attns]
    width = sum(sizes)
    return pl.pallas_call(
        functools.partial(norm_kernel, sizes),
        out_shape=jax.ShapeDtypeStruct((1, rows, width), BF16),
        cost_estimate=pl.CostEstimate(
            flops=3 * rows * width, bytes_accessed=4 * rows * width, transcendentals=0
        ),
        name="row_norm",
    )(*attns, *squares, gain.reshape(1, width))


def swap_halves(pairs):
    return pairs + [(b, a) for a, b in pairs]


def earlier_ctx(part, n_ctx):
    place = lax.axis_index("ctx")
    if n_ctx == 1:
        return jnp.zeros_like(part)
    if n_ctx % 2:
        total = jnp.zeros(part.shape, F32)
        for s in range(1, n_ctx):
            got = lax.ppermute(part, "ctx", [(i, i + s) for i in range(n_ctx - s)])
            total = total + got.astype(F32)
        return total.astype(BF16)
    couples = n_ctx // 2
    odd = place % 2 == 1
    partner = swap_halves([(2 * p, 2 * p + 1) for p in range(couples)])
    other = lax.ppermute(part, "ctx", partner)
    first = jnp.where(odd, other, jnp.zeros_like(other))
    if couples == 1:
        return first
    half = part.shape[0] // 2
    both = part.astype(F32) + other.astype(F32)
    mine = jnp.where(odd, both[half:], both[:half]).astype(BF16)
    before = jnp.zeros(mine.shape, F32)
    for s in range(1, couples):
        pairs = [(i, i + 2 * s) for i in range(n_ctx - 2 * s)]
        if 4 * s >= n_ctx:
            got = lax.ppermute(mine, "ctx", swap_halves(pairs))
            got = jnp.where(place >= 2 * s, got, jnp.zeros_like(got))
        else:
            got = lax.ppermute(mine, "ctx", pairs)
        before = before + got.astype(F32)
    before = before.astype(BF16)
    theirs = lax.ppermute(before, "ctx", partner)
    low = jnp.where(odd, theirs, before)
    high = jnp.where(odd, before, theirs)
    whole = jnp.concatenate([low, high], axis=0)
    return (whole.astype(F32) + first.astype(F32)).astype(BF16)


def add(*terms):
    total = terms[0].astype(F32)
    for term in terms[1:]:
        total = total + term.astype(F32)
    return total.astype(BF16)


def other_heads(early, upto, n_head):
    place = lax.axis_index("head")
    zero = jnp.zeros_like(early)
    if n_head == 1:
        return zero, zero
    if n_head % 2:
        lower, higher = zero, zero
        for _ in range(n_head - 1):
            lower = lax.ppermute(add(lower, upto), "head", [(i, i + 1) for i in range(n_head - 1)])
            higher = lax.ppermute(add(higher, early), "head", [(i + 1, i) for i in range(n_head - 1)])
        return lower, higher
    mid = n_head // 2
    left = place < mid
    mine = jnp.where(left, upto, early)
    mirror = jnp.where(left, early, upto)
    inward = None
    send = mine
    for t in range(mid - 1):
        got = lax.ppermute(send, "head", [(t, t + 1), (n_head - 1 - t, n_head - 2 - t)])
        inward = got if inward is None else inward + got
        send = add(inward, mine)
    outward = lax.ppermute(send, "head", [(mid - 1, mid), (mid, mid - 1)])
    for t in range(mid - 1, 0, -1):
        got = lax.ppermute(
            add(outward, mirror), "head", [(t, t - 1), (n_head - 1 - t, n_head - t)]
        )
        outward = outward + got
    return (zero if inward is None else inward), outward


def plan(heads):
    if heads % 16:
        return [[heads]]
    u = heads // 8
    return [[u], [2 * u], [2 * u, 2 * u, u]]


def body(n_head, n_ctx, queries, keys, values, gain):
    rows, width = queries.shape[1], queries.shape[2]
    q_rows = queries.reshape(rows, width)
    k_rows = keys.reshape(rows, width)
    v_rows = values.reshape(rows, width)
    heads = width // DH
    groups = plan(heads)
    step = heads if len(groups) == 1 else heads // 8
    attns, squares = [], []
    at = 0
    for sizes in groups:
        count = sum(sizes)
        own = kv_states(k_rows, v_rows, at, count, step)
        early = earlier_ctx(own, n_ctx)
        off = 0
        for size in sizes:
            e = early[off : off + size]
            upto = add(e, own[off : off + size])
            inward, outward = other_heads(e, upto, n_head)
            qa, part = local_parts(q_rows, k_rows, v_rows, at + off, size, step)
            attn, sq = attend(qa, part, inward, outward, e)
            attns.append(attn)
            squares.append(sq)
            off += size
        at += count
    return row_norm(attns, squares, gain)


def solution(mesh):
    n_head, n_ctx = mesh.shape["head"], mesh.shape["ctx"]
    return jax.shard_map(
        functools.partial(body, n_head, n_ctx),
        mesh=mesh,
        in_specs=(
            P(("rep", "ctx"), "head", None),
            P(("rep", "ctx"), "head", None),
            P(("rep", "ctx"), "head", None),
            P(),
        ),
        out_specs=P(("rep", "ctx"), "head", None),
        check_vma=False,
    )
```

```python
import functools

import jax
import jax.numpy as jnp
from jax import lax
from jax.experimental import pallas as pl
from jax.experimental.pallas import tpu as pltpu
from jax.sharding import PartitionSpec as P

DH = 128
F32 = jnp.float32
BF16 = jnp.bfloat16
VMEM_LIMIT = 8 << 20
VMEM = pl.BlockSpec(memory_space=pltpu.VMEM)
ANY = pl.BlockSpec(memory_space=pl.ANY)


def silu(x):
    x = x.astype(F32)
    return (x * (0.5 * jnp.tanh(0.5 * x) + 0.5)).astype(BF16)


def call(kernel, name, operands, outs, after):
    n_in, n_after = len(operands), len(after)

    def run(*refs):
        kernel(refs[:n_in], refs[n_in + n_after :])

    return pl.pallas_call(
        run,
        in_specs=[VMEM] * n_in + [ANY] * n_after,
        out_specs=[VMEM] * len(outs),
        out_shape=outs,
        compiler_params=pltpu.CompilerParams(vmem_limit_bytes=VMEM_LIMIT),
        cost_estimate=pl.CostEstimate(flops=1, bytes_accessed=1, transcendentals=0),
        name=name,
    )(*operands, *after)


def head_cols(h):
    return slice(h * DH, (h + 1) * DH)


def states_of(count, rows, kind=BF16):
    return jax.ShapeDtypeStruct((count, rows, DH), kind)


def kv_states(k_rows, v_rows, first, count, after):
    rows = k_rows.shape[0]

    def kernel(ins, outs):
        k_ref, v_ref = ins
        c_ref, ka_ref = outs
        for h in range(count):
            ka = silu(k_ref[:, head_cols(first + h)])
            ka_ref[:, head_cols(h)] = ka
            c_ref[h] = lax.dot_general(
                ka, v_ref[:, head_cols(first + h)], (((0,), (0,)), ((), ())),
                preferred_element_type=F32,
            ).astype(BF16)

    outs = [states_of(count, DH), jax.ShapeDtypeStruct((rows, count * DH), BF16)]
    return call(
        kernel, "kv_states", [k_rows, v_rows], outs, after
    )


def places_block():
    odd = lax.rem(lax.axis_index("ctx"), 2)
    along = lax.axis_index("head")
    rows = lax.broadcasted_iota(jnp.int32, (8, DH), 0)
    left = jnp.where(along < 2, 1, 0)
    outer = jnp.where((along == 0) | (along == 3), 1, 0)
    value = jnp.where(rows == 0, odd, jnp.where(rows == 1, left, outer))
    return value.astype(F32)


def first_kv_states(k_rows, v_rows, count):
    rows = k_rows.shape[0]

    def kernel(k_ref, v_ref, c_ref, ka_ref, m_ref):
        m_ref[...] = places_block()
        for h in range(count):
            ka = silu(k_ref[:, head_cols(h)])
            ka_ref[:, head_cols(h)] = ka
            c_ref[h] = lax.dot_general(
                ka, v_ref[:, head_cols(h)], (((0,), (0,)), ((), ())),
                preferred_element_type=F32,
            ).astype(BF16)

    block = pl.BlockSpec((rows, count * DH), lambda i: (0, 0))
    return pl.pallas_call(
        kernel,
        grid=(1,),
        in_specs=[block, block],
        out_specs=[VMEM, VMEM, VMEM],
        out_shape=[
            states_of(count, DH),
            jax.ShapeDtypeStruct((rows, count * DH), BF16),
            jax.ShapeDtypeStruct((8, DH), F32),
        ],
        compiler_params=pltpu.CompilerParams(vmem_limit_bytes=VMEM_LIMIT),
        cost_estimate=pl.CostEstimate(
            flops=2 * count * rows * DH * DH,
            bytes_accessed=8 * count * rows * DH,
            transcendentals=count * rows * DH,
        ),
        name="first_kv_states",
    )(k_rows, v_rows)


def early_states(other, parts, sizes, after):
    half = other.shape[0] // 2

    def kernel(ins, outs):
        place = lax.axis_index("ctx")
        odd, later = lax.rem(place, 2) == 1, place >= 2
        at = 0
        for f_ref, size in zip(outs, sizes):
            for h in range(size):
                g = at + h
                early = jnp.where(odd, ins[0][g].astype(F32), 0.0)
                if parts:
                    a, b = (ins[1], ins[2]) if g < half else (ins[2], ins[1])
                    i = g if g < half else g - half
                    before = jnp.where(odd, b[i].astype(F32), a[i].astype(F32))
                    early = early + jnp.where(later, before, 0.0)
                f_ref[h] = early.astype(BF16)
            at += size

    outs = [states_of(size, DH) for size in sizes]
    return call(kernel, "early_states", [other, *parts], outs, after)


def total(*terms):
    out = terms[0].astype(F32)
    for term in terms[1:]:
        out = out + term.astype(F32)
    return out


def local_scores(q_rows, ka, first, ka_first, count, after):
    rows = q_rows.shape[0]

    def kernel(ins, outs):
        q_ref, ka_ref = ins
        causal = lax.broadcasted_iota(jnp.int32, (rows, rows), 0) >= lax.broadcasted_iota(
            jnp.int32, (rows, rows), 1
        )
        for h in range(count):
            qa = silu(q_ref[:, head_cols(first + h)])
            scores = lax.dot_general(
                qa, ka_ref[:, head_cols(ka_first + h)], (((1,), (1,)), ((), ())),
                preferred_element_type=F32,
            )
            at = h * (rows + DH)
            outs[0][:, at : at + rows] = jnp.where(causal, scores, 0.0).astype(BF16)
            outs[0][:, at + rows : at + rows + DH] = qa

    out = jax.ShapeDtypeStruct((rows, count * (rows + DH)), BF16)
    return call(
        kernel, "local_scores", [q_rows, ka], [out], after
    )[0]


def attend_head(both_ref, v, terms, h, rows):
    at = h * (rows + DH)
    state = terms[0][h].astype(F32)
    for ref in terms[1:]:
        state = state + ref[h].astype(F32)
    right = jnp.concatenate([v, state.astype(BF16)], axis=0)
    return jnp.dot(
        both_ref[:, at : at + rows + DH], right, preferred_element_type=F32
    ).astype(BF16)


def attend(both, v_rows, first, terms, after):
    rows = both.shape[0]
    count = both.shape[1] // (rows + DH)

    def kernel(ins, outs):
        both_ref, v_ref, terms = ins[0], ins[1], ins[2:]
        total = None
        for h in range(count):
            attn = attend_head(both_ref, v_ref[:, head_cols(first + h)], terms, h, rows)
            outs[0][:, head_cols(h)] = attn
            wide = attn.astype(F32)
            total = wide * wide if total is None else total + wide * wide
        outs[1][...] = total

    outs = [
        jax.ShapeDtypeStruct((rows, count * DH), BF16),
        jax.ShapeDtypeStruct((rows, DH), F32),
    ]
    return call(
        kernel, "attend", [both, v_rows, *terms], outs, after
    )


def last_attend(both, v_rows, first, terms, attns, squares, gain):
    rows, width = v_rows.shape
    count = both.shape[1] // (rows + DH)
    n_terms, n = len(terms), len(attns)
    starts, at = [], 0
    for a in attns:
        starts.append(at)
        at += a.shape[1]

    def kernel(ins, outs):
        both_ref, v_ref = ins[0], ins[1]
        terms = ins[2 : 2 + n_terms]
        attn_refs = ins[2 + n_terms : 2 + n_terms + n]
        sq_refs = ins[2 + n_terms + n : 2 + n_terms + 2 * n]
        gain_ref, out_ref = ins[-1], outs[0]
        total = None
        for ref in sq_refs:
            total = ref[...] if total is None else total + ref[...]
        last = []
        for h in range(count):
            attn = attend_head(both_ref, v_ref[:, head_cols(first + h)], terms, h, rows)
            last.append(attn)
            wide = attn.astype(F32)
            total = wide * wide if total is None else total + wide * wide
        mean_sq = jnp.sum(total, axis=1, keepdims=True) / width
        scale = jnp.broadcast_to(lax.rsqrt(mean_sq + 1e-06), (rows, DH))
        for ref, start in zip(attn_refs, starts):
            for h in range(ref.shape[1] // DH):
                cols = slice(start + h * DH, start + (h + 1) * DH)
                out_ref[0, :, cols] = (
                    ref[:, head_cols(h)].astype(F32) * scale * gain_ref[:, cols]
                ).astype(BF16)
        for h in range(count):
            cols = head_cols(first + h)
            out_ref[0, :, cols] = (
                last[h].astype(F32) * scale * gain_ref[:, cols]
            ).astype(BF16)

    out = jax.ShapeDtypeStruct((1, rows, width), BF16)
    return call(
        kernel, "last_attend",
        [both, v_rows, *terms, *attns, *squares, gain.reshape(1, width)], [out], [],
    )[0]


def held(x, after):
    return lax.optimization_barrier((x, *after))[0]


def both_ways(pairs):
    return pairs + [(b, a) for a, b in pairs]


class Group:
    def __init__(self, n_ctx, first, sizes):
        self.n_ctx = n_ctx
        self.first, self.sizes, self.count = first, sizes, sum(sizes)
        self.partner = both_ways([(2 * p, 2 * p + 1) for p in range(n_ctx // 2)])
        self.got = []

    def begin(self, own, ka, odd):
        self.own, self.ka, self.odd = own, ka, odd
        if self.n_ctx % 2 == 0:
            self.other = lax.ppermute(own, "ctx", self.partner)
        return [own]

    def cross(self, after):
        n = self.n_ctx
        if n == 2 or n % 2:
            return after
        half = self.count // 2
        own, other = self.own, held(self.other, after)
        mine = jnp.where(
            self.odd, total(own[half:], other[half:]), total(own[:half], other[:half])
        ).astype(BF16)
        for s in range(1, n // 2):
            pairs = [(i, i + 2 * s) for i in range(n - 2 * s)]
            self.got.append(lax.ppermute(mine, "ctx", both_ways(pairs) if n == 4 else pairs))
        return [mine]

    def spread(self, after):
        n = self.n_ctx
        if n == 2 or n % 2:
            return after
        got = self.got[0] if n == 4 else total(*self.got).astype(BF16)
        self.got = [held(got, after)]
        self.theirs = lax.ppermute(self.got[0], "ctx", self.partner)
        return self.got

    def finish(self, after):
        n = self.n_ctx
        parts = []
        if n == 1:
            return [jnp.zeros_like(self.own)]
        if n % 2:
            got = [
                lax.ppermute(self.own, "ctx", [(i, i + s) for i in range(n - s)])
                for s in range(1, n)
            ]
            return [total(*got).astype(BF16)]
        if n > 2:
            parts = [self.got[0], self.theirs]
        return early_states(self.other, parts, self.sizes, after)


def whole_chain(n_head, own, early):
    upto = total(early, own)
    early = early.astype(F32)
    left = lax.axis_index("head") < n_head // 2
    if n_head == 1:
        return early.astype(BF16)
    if n_head % 2:
        lower = higher = jnp.zeros_like(own)
        for _ in range(n_head - 1):
            lower = lax.ppermute(
                total(lower, upto).astype(BF16), "head", [(i, i + 1) for i in range(n_head - 1)]
            )
            higher = lax.ppermute(
                total(higher, early).astype(BF16), "head", [(i + 1, i) for i in range(n_head - 1)]
            )
        return total(early, lower, higher).astype(BF16)
    mid = n_head // 2
    mine, mirror = jnp.where(left, upto, early), jnp.where(left, early, upto)
    inward = jnp.zeros_like(own)
    for t in range(mid - 1):
        inward = inward + lax.ppermute(
            total(inward, mine).astype(BF16), "head", [(t, t + 1), (n_head - 1 - t, n_head - 2 - t)]
        )
    outward = lax.ppermute(total(inward, mine).astype(BF16), "head", both_ways([(mid - 1, mid)]))
    for t in range(mid - 1, 0, -1):
        outward = outward + lax.ppermute(
            total(outward, mirror).astype(BF16), "head", [(t, t - 1), (n_head - 1 - t, n_head - t)]
        )
    return total(early, inward, outward).astype(BF16)


SKEW = 3


class Four:
    def __init__(self, n_ctx, n, masks):
        self.n, self.n_ctx = n, n_ctx
        self.left, self.outer = masks[1] > 0, masks[2] > 0
        self.own, self.early, self.a, self.b = {}, {}, {}, {}
        at = lambda z, c: z * n_ctx + c
        self.swap = both_ways([(1, 2)])
        if n_ctx % 2 == 0:
            self.swap = both_ways(
                [(at(1, c), at(2, c)) for c in range(n_ctx)]
                + [(at(z, c), at(z, c + 1)) for z in (0, 3) for c in range(0, n_ctx, 2)]
            )

    def mine(self, c):
        f = self.early[c].astype(F32)
        return f + jnp.where(self.left, self.own[c].astype(F32), 0.0)

    def mirror(self, c):
        f = self.early[c].astype(F32)
        return f + jnp.where(self.left, 0.0, self.own[c].astype(F32))

    def side(self, t, after):
        inwards, outwards = t < self.n, t >= SKEW
        c = t - SKEW
        if outwards:
            out = total(self.b[c], self.mirror(c))
        if inwards and outwards:
            send = jnp.where(self.outer, self.mine(t), out)
        else:
            send = self.mine(t) if inwards else out
        send = held(send.astype(BF16), after)
        self.a[t] = lax.ppermute(send, "head", both_ways([(0, 1), (3, 2)]))
        return [send]

    def middle(self, t, after):
        send = held(total(self.a[t], self.mine(t)).astype(BF16), after)
        axes = ("head", "ctx") if self.n_ctx % 2 == 0 else "head"
        self.b[t] = lax.ppermute(send, axes, self.swap)
        return [send]

    def state(self, c, after):
        got = jnp.where(
            self.outer, self.a[c + SKEW].astype(F32), total(self.a[c], self.b[c])
        )
        return held((got + self.early[c].astype(F32)).astype(BF16), after)


def plan(heads, n_head):
    if n_head != 4 or heads % 16:
        return [[heads]]
    u = heads // 8
    return [[u], [u], [u, u], [u, u, u, u]]


def body(n_head, n_ctx, queries, keys, values, gain):
    rows, width = queries.shape[1], queries.shape[2]
    q_rows = queries.reshape(rows, width)
    k_rows = keys.reshape(rows, width)
    v_rows = values.reshape(rows, width)
    heads = width // DH
    groups, chunks = [], []
    for sizes in plan(heads, n_head):
        g = Group(n_ctx, len(chunks) and sum(c[2] for c in chunks), sizes)
        groups.append(g)
        for i, size in enumerate(sizes):
            chunks.append((g, g.first + sum(sizes[:i]), size))
    n = len(chunks)
    both, states, attns, squares = {}, {}, {}, {}

    masks = None

    def kv(g, after):
        odd = masks[0] > 0 if masks is not None else lax.axis_index("ctx") % 2 == 1
        return g.begin(*kv_states(k_rows, v_rows, g.first, g.count, after), odd)

    def scores(c, after):
        g, first, size = chunks[c]
        both[c] = local_scores(q_rows, g.ka, first, first - g.first, size, after)
        return [both[c]]

    def attention(c, after):
        attns[c], squares[c] = attend(both[c], v_rows, chunks[c][1], [states[c]], after)
        return [squares[c]]

    if n == 1:
        g = groups[0]
        clock = kv(g, [])
        clock = g.cross(clock)
        clock = g.spread(clock)
        early = g.finish(clock)[0]
        states[0] = whole_chain(n_head, g.own, early)
        scores(0, [])
    else:
        def ready(g, after):
            early = g.finish(after)
            at = 0
            for c in range(n):
                if chunks[c][0] is g:
                    four.early[c] = early[at]
                    first = chunks[c][1] - g.first
                    four.own[c] = g.own[first : first + chunks[c][2]]
                    at += 1
            return [early[0]]

        g0, g1, g2, g3 = groups
        own, ka, masks = first_kv_states(k_rows, v_rows, g0.count)
        four = Four(n_ctx, n, masks)
        clock = g0.begin(own, ka, masks[0] > 0)
        clock = kv(g1, clock)
        clock = g0.cross(clock)
        clock = kv(g2, clock)
        clock = g1.cross(clock)
        clock = kv(g3, clock)
        clock = scores(0, clock)
        clock = g0.spread(clock)
        clock = g2.cross(clock)
        clock = ready(g0, clock)
        clock = four.side(0, clock)
        clock = scores(1, clock)
        clock = g1.spread(clock)
        clock = g3.cross(clock)
        clock = ready(g1, clock)
        clock = four.side(1, clock)
        clock = scores(2, clock)
        clock = four.middle(0, clock)
        clock = g2.spread(clock)
        clock = scores(3, clock)
        clock = ready(g2, clock)
        for t in range(2, n + SKEW):
            clock = four.side(t, clock)
            if t + 2 < n:
                clock = scores(t + 2, clock)
            c = t - 1 - SKEW
            if c >= 0:
                states[c] = four.state(c, clock)
                clock = attention(c, [states[c]])
            if t == 2:
                clock = g3.spread(clock)
                clock = ready(g3, clock)
            if t - 1 < n:
                clock = four.middle(t - 1, clock)
            if 0 <= t - 2 < n:
                clock = [held(four.b[t - 2], clock)]
                four.b[t - 2] = clock[0]
        states[n - 1] = four.state(n - 1, clock)
    return last_attend(
        both[n - 1], v_rows, chunks[n - 1][1], [states[n - 1]],
        [attns[c] for c in range(n - 1)], [squares[c] for c in range(n - 1)], gain,
    )


def solution(mesh):
    n_head, n_ctx = mesh.shape["head"], mesh.shape["ctx"]
    return jax.shard_map(
        functools.partial(body, n_head, n_ctx),
        mesh=mesh,
        in_specs=(
            P(("rep", "ctx"), "head", None),
            P(("rep", "ctx"), "head", None),
            P(("rep", "ctx"), "head", None),
            P(),
        ),
        out_specs=P(("rep", "ctx"), "head", None),
        check_vma=False,
    )
```

```python
import functools

import jax
import jax.numpy as jnp
from jax import lax
from jax.experimental import pallas as pl
from jax.experimental.pallas import tpu as pltpu
from jax.sharding import PartitionSpec as P

DH = 128
F32 = jnp.float32
BF16 = jnp.bfloat16
VMEM_LIMIT = 8 << 20
COST = 2 * 10**9
VMEM = pl.BlockSpec(memory_space=pltpu.VMEM)
ANY = pl.BlockSpec(memory_space=pl.ANY)


def silu(x):
    x = x.astype(F32)
    return (x * (0.5 * jnp.tanh(0.5 * x) + 0.5)).astype(BF16)


def call(kernel, name, operands, outs, after):
    n_in, n_after = len(operands), len(after)

    def run(*refs):
        kernel(refs[:n_in], refs[n_in + n_after :])

    return pl.pallas_call(
        run,
        in_specs=[VMEM] * n_in + [ANY] * n_after,
        out_specs=[VMEM] * len(outs),
        out_shape=outs,
        compiler_params=pltpu.CompilerParams(vmem_limit_bytes=VMEM_LIMIT),
        cost_estimate=pl.CostEstimate(flops=COST, bytes_accessed=1, transcendentals=0),
        name=name,
    )(*operands, *after)


def head_cols(h):
    return slice(h * DH, (h + 1) * DH)


def states_of(count, rows, kind=BF16):
    return jax.ShapeDtypeStruct((count, rows, DH), kind)


def kv_states(k_rows, v_rows, first, count, after):
    rows = k_rows.shape[0]

    def kernel(ins, outs):
        k_ref, v_ref = ins
        c_ref, ka_ref = outs
        for h in range(count):
            ka = silu(k_ref[:, head_cols(first + h)])
            ka_ref[:, head_cols(h)] = ka
            c_ref[h] = lax.dot_general(
                ka, v_ref[:, head_cols(first + h)], (((0,), (0,)), ((), ())),
                preferred_element_type=F32,
            ).astype(BF16)

    outs = [states_of(count, DH), jax.ShapeDtypeStruct((rows, count * DH), BF16)]
    return call(
        kernel, "kv_states", [k_rows, v_rows], outs, after
    )


def places_block():
    place = lax.axis_index("ctx")
    odd = lax.rem(place, 2)
    later = jnp.where(place >= 2, 1, 0)
    along = lax.axis_index("head")
    rows = lax.broadcasted_iota(jnp.int32, (8, DH), 0)
    left = jnp.where(along < 2, 1, 0)
    outer = jnp.where((along == 0) | (along == 3), 1, 0)
    value = jnp.where(rows == 0, odd, jnp.where(rows == 1, left, jnp.where(rows == 2, outer, later)))
    return value.astype(F32)


def first_kv_states(k_rows, v_rows, count):
    rows = k_rows.shape[0]

    def kernel(k_ref, v_ref, c_ref, ka_ref, m_ref):
        m_ref[...] = places_block()
        for h in range(count):
            ka = silu(k_ref[:, head_cols(h)])
            ka_ref[:, head_cols(h)] = ka
            c_ref[h] = lax.dot_general(
                ka, v_ref[:, head_cols(h)], (((0,), (0,)), ((), ())),
                preferred_element_type=F32,
            ).astype(BF16)

    block = pl.BlockSpec((rows, count * DH), lambda i: (0, 0))
    return pl.pallas_call(
        kernel,
        grid=(1,),
        in_specs=[block, block],
        out_specs=[VMEM, VMEM, VMEM],
        out_shape=[
            states_of(count, DH),
            jax.ShapeDtypeStruct((rows, count * DH), BF16),
            jax.ShapeDtypeStruct((8, DH), F32),
        ],
        compiler_params=pltpu.CompilerParams(vmem_limit_bytes=VMEM_LIMIT),
        cost_estimate=pl.CostEstimate(
            flops=2 * count * rows * DH * DH,
            bytes_accessed=8 * count * rows * DH,
            transcendentals=count * rows * DH,
        ),
        name="first_kv_states",
    )(k_rows, v_rows)


def total(*terms):
    out = terms[0].astype(F32)
    for term in terms[1:]:
        out = out + term.astype(F32)
    return out


def local_scores(q_rows, ka, ka_first, first, count, after):
    rows = q_rows.shape[0]

    def kernel(ins, outs):
        q_ref, ka_ref = ins
        causal = lax.broadcasted_iota(jnp.int32, (rows, rows), 0) >= lax.broadcasted_iota(
            jnp.int32, (rows, rows), 1
        )
        for h in range(count):
            qa = silu(q_ref[:, head_cols(first + h)])
            scores = lax.dot_general(
                qa, ka_ref[:, head_cols(ka_first + h)], (((1,), (1,)), ((), ())),
                preferred_element_type=F32,
            )
            at = h * (rows + DH)
            outs[0][:, at : at + rows] = jnp.where(causal, scores, 0.0).astype(BF16)
            outs[0][:, at + rows : at + rows + DH] = qa

    out = jax.ShapeDtypeStruct((rows, count * (rows + DH)), BF16)
    return call(
        kernel, "local_scores", [q_rows, ka], [out], after
    )[0]


def attend_head(both_ref, v, terms, h, rows):
    at = h * (rows + DH)
    state = terms[0][h].astype(F32)
    for ref in terms[1:]:
        state = state + ref[h].astype(F32)
    right = jnp.concatenate([v, state.astype(BF16)], axis=0)
    return jnp.dot(
        both_ref[:, at : at + rows + DH], right, preferred_element_type=F32
    ).astype(BF16)


def attend(both, v_rows, first, terms, after):
    rows = both.shape[0]
    count = both.shape[1] // (rows + DH)

    def kernel(ins, outs):
        both_ref, v_ref, terms = ins[0], ins[1], ins[2:]
        total = None
        for h in range(count):
            attn = attend_head(both_ref, v_ref[:, head_cols(first + h)], terms, h, rows)
            outs[0][:, head_cols(h)] = attn
            wide = attn.astype(F32)
            total = wide * wide if total is None else total + wide * wide
        outs[1][...] = total

    outs = [
        jax.ShapeDtypeStruct((rows, count * DH), BF16),
        jax.ShapeDtypeStruct((rows, DH), F32),
    ]
    return call(
        kernel, "attend", [both, v_rows, *terms], outs, after
    )


def last_attend(both, v_rows, first, terms, attns, squares, gain):
    rows, width = v_rows.shape
    count = both.shape[1] // (rows + DH)
    n_terms, n = len(terms), len(attns)
    starts, at = [], 0
    for a in attns:
        starts.append(at)
        at += a.shape[1]

    def kernel(ins, outs):
        both_ref, v_ref = ins[0], ins[1]
        terms = ins[2 : 2 + n_terms]
        attn_refs = ins[2 + n_terms : 2 + n_terms + n]
        sq_refs = ins[2 + n_terms + n : 2 + n_terms + 2 * n]
        gain_ref, out_ref = ins[-1], outs[0]
        total = None
        for ref in sq_refs:
            total = ref[...] if total is None else total + ref[...]
        last = []
        for h in range(count):
            attn = attend_head(both_ref, v_ref[:, head_cols(first + h)], terms, h, rows)
            last.append(attn)
            wide = attn.astype(F32)
            total = wide * wide if total is None else total + wide * wide
        mean_sq = jnp.sum(total, axis=1, keepdims=True) / width
        scale = jnp.broadcast_to(lax.rsqrt(mean_sq + 1e-06), (rows, DH))
        for ref, start in zip(attn_refs, starts):
            for h in range(ref.shape[1] // DH):
                cols = slice(start + h * DH, start + (h + 1) * DH)
                out_ref[0, :, cols] = (
                    ref[:, head_cols(h)].astype(F32) * scale * gain_ref[:, cols]
                ).astype(BF16)
        for h in range(count):
            cols = head_cols(first + h)
            out_ref[0, :, cols] = (
                last[h].astype(F32) * scale * gain_ref[:, cols]
            ).astype(BF16)

    out = jax.ShapeDtypeStruct((1, rows, width), BF16)
    return call(
        kernel, "last_attend",
        [both, v_rows, *terms, *attns, *squares, gain.reshape(1, width)], [out], [],
    )[0]


def held(x, after):
    return lax.optimization_barrier((x, *after))[0]


def both_ways(pairs):
    return pairs + [(b, a) for a, b in pairs]


def before_ctx(n_ctx, own):
    odd = lax.axis_index("ctx") % 2 == 1
    before = jnp.zeros(own.shape, F32)
    if n_ctx % 2:
        for s in range(1, n_ctx):
            before = total(before, lax.ppermute(own, "ctx", [(i, i + s) for i in range(n_ctx - s)]))
        return before.astype(BF16)
    other = lax.ppermute(own, "ctx", both_ways([(i, i + 1) for i in range(0, n_ctx, 2)]))
    couple = total(own, other).astype(BF16)
    for s in range(2, n_ctx, 2):
        before = total(before, lax.ppermute(couple, "ctx", [(i, i + s) for i in range(n_ctx - s)]))
    return (before + jnp.where(odd, other.astype(F32), 0.0)).astype(BF16)


def whole_chain(n_head, own, early):
    upto = total(early, own)
    early = early.astype(F32)
    left = lax.axis_index("head") < n_head // 2
    if n_head == 1:
        return early.astype(BF16)
    if n_head % 2:
        lower = higher = jnp.zeros_like(own)
        for _ in range(n_head - 1):
            lower = lax.ppermute(
                total(lower, upto).astype(BF16), "head", [(i, i + 1) for i in range(n_head - 1)]
            )
            higher = lax.ppermute(
                total(higher, early).astype(BF16), "head", [(i + 1, i) for i in range(n_head - 1)]
            )
        return total(early, lower, higher).astype(BF16)
    mid = n_head // 2
    mine, mirror = jnp.where(left, upto, early), jnp.where(left, early, upto)
    inward = jnp.zeros_like(own)
    for t in range(mid - 1):
        inward = inward + lax.ppermute(
            total(inward, mine).astype(BF16), "head", [(t, t + 1), (n_head - 1 - t, n_head - 2 - t)]
        )
    outward = lax.ppermute(total(inward, mine).astype(BF16), "head", both_ways([(mid - 1, mid)]))
    for t in range(mid - 1, 0, -1):
        outward = outward + lax.ppermute(
            total(outward, mirror).astype(BF16), "head", [(t, t - 1), (n_head - 1 - t, n_head - t)]
        )
    return total(early, inward, outward).astype(BF16)


SKEW = 3


class Scan:
    def __init__(self, n, masks):
        self.n = n
        self.odd, self.left, self.outer, self.later = (masks[i] > 0 for i in range(4))
        self.own, self.other, self.x, self.a, self.b = {}, {}, {}, {}, {}
        self.couples = both_ways([(0, 1), (2, 3)])
        at = lambda z, c: 4 * z + c
        self.swap = both_ways(
            [(at(1, c), at(2, c)) for c in range(4)]
            + [(at(z, c), at(z, c + 1)) for z in (0, 3) for c in (0, 2)]
        )

    def begin(self, own):
        return lax.ppermute(own, "ctx", self.couples)

    def cross(self, c, after):
        send = held(total(self.own[c], self.other[c]).astype(BF16), after)
        self.x[c] = lax.ppermute(send, "ctx", both_ways([(0, 2), (1, 3)]))
        return [send]

    def early(self, c):
        couple = jnp.where(self.odd, self.other[c].astype(F32), 0.0)
        return couple + jnp.where(self.later, self.x[c].astype(F32), 0.0)

    def mine(self, c):
        return self.early(c) + jnp.where(self.left, self.own[c].astype(F32), 0.0)

    def mirror(self, c):
        return self.early(c) + jnp.where(self.left, 0.0, self.own[c].astype(F32))

    def side(self, t, after):
        inwards, outwards = t < self.n, t >= SKEW
        c = t - SKEW
        if inwards:
            self.arrived(self.x, t, after)
        if outwards:
            out = total(self.b[c], self.mirror(c))
        if inwards and outwards:
            send = jnp.where(self.outer, self.mine(t), out)
        else:
            send = self.mine(t) if inwards else out
        send = held(send.astype(BF16), after)
        self.a[t] = lax.ppermute(send, "head", both_ways([(0, 1), (3, 2)]))
        return [send]

    def middle(self, t, after):
        self.arrived(self.a, t, after)
        send = held(total(self.a[t], self.mine(t)).astype(BF16), after)
        self.b[t] = lax.ppermute(send, ("head", "ctx"), self.swap)
        return [send]

    def arrived(self, table, c, after):
        table[c] = held(table[c], after)
        return [table[c]]

    def state(self, c, after):
        self.arrived(self.a, c + SKEW, after)
        got = jnp.where(
            self.outer, self.a[c + SKEW].astype(F32), total(self.a[c], self.b[c])
        )
        return held((got + self.early(c)).astype(BF16), after)


def body(n_head, n_ctx, queries, keys, values, gain):
    rows, width = queries.shape[1], queries.shape[2]
    q_rows = queries.reshape(rows, width)
    k_rows = keys.reshape(rows, width)
    v_rows = values.reshape(rows, width)
    heads = width // DH
    if n_head != 4 or n_ctx != 4 or heads % 8:
        own, ka = kv_states(k_rows, v_rows, 0, heads, [])
        state = whole_chain(n_head, own, before_ctx(n_ctx, own))
        both = local_scores(q_rows, ka, 0, 0, heads, [])
        return last_attend(both, v_rows, 0, [state], [], [], gain)

    n = 8
    size = heads // n
    both, states, attns, squares, ka = {}, {}, {}, {}, {}

    own, keys_active, masks = first_kv_states(k_rows, v_rows, size)
    scan = Scan(n, masks)

    def begin(first, count, own, keys_active):
        other = scan.begin(own)
        for i in range(count):
            c = first + i
            cut = slice(i * size, (i + 1) * size)
            scan.own[c], scan.other[c] = own[cut], other[cut]
            ka[c] = (keys_active, i * size)
        return [own]

    def kv(first, count, after):
        return begin(
            first, count, *kv_states(k_rows, v_rows, first * size, count * size, after)
        )

    def scores(c, after):
        both[c] = local_scores(q_rows, *ka[c], c * size, size, after)
        return [both[c]]

    def attention(c, after):
        attns[c], squares[c] = attend(both[c], v_rows, c * size, [states[c]], after)
        return [squares[c]]

    clock = begin(0, 1, own, keys_active)
    clock = kv(1, 1, clock)
    clock = scan.cross(0, clock)
    clock = scan.cross(1, clock)
    clock = kv(2, 2, clock)
    clock = kv(4, 4, clock)
    clock = scores(0, clock)
    clock = scores(1, clock)
    for t in range(n + SKEW):
        clock = scan.side(t, clock)
        if t + 2 < n:
            clock = scores(t + 2, clock)
        if 0 <= t - 1 < n:
            clock = scan.middle(t - 1, clock)
        if t + 2 < n:
            clock = scan.cross(t + 2, clock)
        c = t - 1 - SKEW
        if c >= 0:
            states[c] = scan.state(c, clock)
            clock = attention(c, [states[c]])
        if 0 <= t - 2 < n:
            clock = scan.arrived(scan.b, t - 2, clock)
    states[n - 1] = scan.state(n - 1, clock)
    return last_attend(
        both[n - 1], v_rows, (n - 1) * size, [states[n - 1]],
        [attns[c] for c in range(n - 1)], [squares[c] for c in range(n - 1)], gain,
    )


def solution(mesh):
    n_head, n_ctx = mesh.shape["head"], mesh.shape["ctx"]
    return jax.shard_map(
        functools.partial(body, n_head, n_ctx),
        mesh=mesh,
        in_specs=(
            P(("rep", "ctx"), "head", None),
            P(("rep", "ctx"), "head", None),
            P(("rep", "ctx"), "head", None),
            P(),
        ),
        out_specs=P(("rep", "ctx"), "head", None),
        check_vma=False,
    )
```

```python
import functools

import jax
import jax.numpy as jnp
from jax import lax
from jax.experimental import pallas as pl
from jax.experimental.pallas import tpu as pltpu
from jax.sharding import PartitionSpec as P

DH = 128
F32 = jnp.float32
BF16 = jnp.bfloat16
VMEM_LIMIT = 8 << 20
PART = 4
COST = 2 * 10**9
VMEM = pl.BlockSpec(memory_space=pltpu.VMEM)
ANY = pl.BlockSpec(memory_space=pl.ANY)


def silu(x):
    x = x.astype(F32)
    return (x * (0.5 * jnp.tanh(0.5 * x) + 0.5)).astype(BF16)


def call(kernel, name, operands, outs, after):
    n_in, n_after = len(operands), len(after)

    def run(*refs):
        kernel(refs[:n_in], refs[n_in + n_after :])

    return pl.pallas_call(
        run,
        in_specs=[VMEM] * n_in + [ANY] * n_after,
        out_specs=[VMEM] * len(outs),
        out_shape=outs,
        compiler_params=pltpu.CompilerParams(vmem_limit_bytes=VMEM_LIMIT),
        cost_estimate=pl.CostEstimate(flops=COST, bytes_accessed=1, transcendentals=0),
        name=name,
    )(*operands, *after)


def head_cols(h):
    return slice(h * DH, (h + 1) * DH)


def states_of(count, rows, kind=BF16):
    return jax.ShapeDtypeStruct((count, rows, DH), kind)


def conditions():
    place, along = lax.axis_index("ctx"), lax.axis_index("head")
    outer = (along == 0) | (along == 3)
    return {
        "odd": lax.rem(place, 2) == 1,
        "even": lax.rem(place, 2) == 0,
        "later": place >= 2,
        "left": along < 2,
        "right": along >= 2,
        "outer": outer,
        "inner": jnp.logical_not(outer),
    }


def term_sum(refs, terms, held, h):
    out = None
    for ref, (_, first, wanted) in zip(refs, terms):
        x = ref[first + h].astype(F32)
        if wanted:
            x = jnp.where(held[wanted], x, 0.0)
        out = x if out is None else out + x
    return out


def combine(name, count, chunks, after):
    starts = [sum(len(c) for c in chunks[:i]) for i in range(len(chunks))]

    def kernel(ins, outs):
        held = Held()
        for i, terms in enumerate(chunks):
            for h in range(count):
                outs[0][i * count + h] = term_sum(ins[starts[i] :], terms, held, h).astype(BF16)

    arrays = [t[0] for terms in chunks for t in terms]
    return call(kernel, name, arrays, [states_of(count * len(chunks), DH)], after)[0]


class Held:
    def __init__(self):
        self.base, self.known = conditions(), {}

    def __getitem__(self, wanted):
        if wanted not in self.known:
            out = self.base[wanted[0]]
            for name in wanted[1:]:
                out = out & self.base[name]
            self.known[wanted] = out
        return self.known[wanted]


def kv_states(k_rows, v_rows, first, count, after, limit=VMEM_LIMIT):
    rows = k_rows.shape[0]
    n_after = len(after)

    def run(*refs):
        k_hbm, v_hbm = refs[:2]
        outs = refs[2 + n_after : -3]
        k_ref, v_ref, sem = refs[-3:]
        parts = count // PART
        copies = []
        for i in range(parts):
            cols = pl.ds((first + i * PART) * DH, PART * DH)
            to = pl.ds(i * PART * DH, PART * DH)
            for j, (hbm_ref, ref) in enumerate(((k_hbm, k_ref), (v_hbm, v_ref))):
                copy = pltpu.make_async_copy(hbm_ref.at[:, cols], ref.at[:, to], sem.at[2 * i + j])
                copy.start()
                copies.append(copy)
        for h in range(count):
            if h % PART == 0:
                copies[2 * (h // PART)].wait()
                copies[2 * (h // PART) + 1].wait()
            ka = silu(k_ref[:, head_cols(h)])
            outs[1][:, head_cols(h)] = ka
            outs[0][h] = lax.dot_general(
                ka, v_ref[:, head_cols(h)], (((0,), (0,)), ((), ())),
                preferred_element_type=F32,
            ).astype(BF16)

    outs = [states_of(count, DH), jax.ShapeDtypeStruct((rows, count * DH), BF16)]
    hbm = pl.BlockSpec(memory_space=pltpu.HBM)
    block = pltpu.VMEM((rows, count * DH), BF16)
    return pl.pallas_call(
        run,
        in_specs=[hbm, hbm] + [ANY] * n_after,
        out_specs=[VMEM] * len(outs),
        out_shape=outs,
        scratch_shapes=[block, block, pltpu.SemaphoreType.DMA((2 * (count // PART),))],
        compiler_params=pltpu.CompilerParams(vmem_limit_bytes=limit),
        cost_estimate=pl.CostEstimate(flops=10**6, bytes_accessed=1, transcendentals=0),
        name="kv_states",
    )(k_rows, v_rows, *after)


def local_scores(q_rows, ka, ka_first, first, count, after):
    rows = q_rows.shape[0]

    def kernel(ins, outs):
        q_ref, ka_ref = ins
        causal = lax.broadcasted_iota(jnp.int32, (rows, rows), 0) >= lax.broadcasted_iota(
            jnp.int32, (rows, rows), 1
        )
        for h in range(count):
            qa = silu(q_ref[:, head_cols(first + h)])
            scores = lax.dot_general(
                qa, ka_ref[:, head_cols(ka_first + h)], (((1,), (1,)), ((), ())),
                preferred_element_type=F32,
            )
            at = h * (rows + DH)
            outs[0][:, at : at + rows] = jnp.where(causal, scores, 0.0).astype(BF16)
            outs[0][:, at + rows : at + rows + DH] = qa

    out = jax.ShapeDtypeStruct((rows, count * (rows + DH)), BF16)
    return call(
        kernel, "local_scores", [q_rows, ka], [out], after
    )[0]


def attend_head(both_ref, v, state, h, rows):
    at = h * (rows + DH)
    right = jnp.concatenate([v, state.astype(BF16)], axis=0)
    return jnp.dot(
        both_ref[:, at : at + rows + DH], right, preferred_element_type=F32
    ).astype(BF16)


def attend(both, v_rows, first, terms, after):
    rows = both.shape[0]
    count = both.shape[1] // (rows + DH)

    def kernel(ins, outs):
        both_ref, v_ref, refs = ins[0], ins[1], ins[2:]
        held = Held()
        squares = None
        for h in range(count):
            state = term_sum(refs, terms, held, h)
            attn = attend_head(both_ref, v_ref[:, head_cols(first + h)], state, h, rows)
            outs[0][:, head_cols(h)] = attn
            wide = attn.astype(F32)
            squares = wide * wide if squares is None else squares + wide * wide
        outs[1][...] = squares

    outs = [
        jax.ShapeDtypeStruct((rows, count * DH), BF16),
        jax.ShapeDtypeStruct((rows, DH), F32),
    ]
    return call(kernel, "attend", [both, v_rows, *(t[0] for t in terms)], outs, after)


def last_attend(both, v_rows, first, terms, attns, squares, gain):
    rows, width = v_rows.shape
    count = both.shape[1] // (rows + DH)
    n_terms, n = len(terms), len(attns)
    starts = [0]
    for a in attns:
        starts.append(starts[-1] + a.shape[1])

    def kernel(*refs):
        both_ref, v_ref = refs[:2]
        term_refs = refs[2 : 2 + n_terms]
        attn_refs = refs[2 + n_terms : 2 + n_terms + n]
        sq_refs = refs[2 + n_terms + n : 2 + n_terms + 2 * n]
        gain_ref, out_hbm, done_ref, sem = refs[2 + n_terms + 2 * n :]
        held = Held()
        squares = None
        last = []
        for h in range(count):
            state = term_sum(term_refs, terms, held, h)
            attn = attend_head(both_ref, v_ref[:, head_cols(first + h)], state, h, rows)
            last.append(attn)
            wide = attn.astype(F32)
            squares = wide * wide if squares is None else squares + wide * wide
        for ref in sq_refs:
            squares = squares + ref[...]
        mean_sq = jnp.sum(squares, axis=1, keepdims=True) / width
        scale = jnp.broadcast_to(lax.rsqrt(mean_sq + 1e-06), (rows, DH))
        copies = []
        for i, start in enumerate(starts):
            wide = count * DH if i == n else attn_refs[i].shape[1]
            for h in range(wide // DH):
                cols = slice(start + h * DH, start + (h + 1) * DH)
                attn = last[h] if i == n else attn_refs[i][:, head_cols(h)]
                done_ref[:, cols] = (attn.astype(F32) * scale * gain_ref[:, cols]).astype(BF16)
            part = pl.ds(start, wide)
            copy = pltpu.make_async_copy(
                done_ref.at[:, part], out_hbm.at[0, :, part], sem.at[i]
            )
            copy.start()
            copies.append(copy)
        for copy in copies:
            copy.wait()

    operands = [both, v_rows, *(t[0] for t in terms), *attns, *squares, gain.reshape(1, width)]
    return pl.pallas_call(
        kernel,
        in_specs=[VMEM] * len(operands),
        out_specs=pl.BlockSpec(memory_space=pltpu.HBM),
        out_shape=jax.ShapeDtypeStruct((1, rows, width), BF16),
        scratch_shapes=[pltpu.VMEM((rows, width), BF16), pltpu.SemaphoreType.DMA((n + 1,))],
        compiler_params=pltpu.CompilerParams(vmem_limit_bytes=VMEM_LIMIT),
        cost_estimate=pl.CostEstimate(flops=COST, bytes_accessed=1, transcendentals=0),
        name="last_attend",
    )(*operands)


def total(*terms):
    out = terms[0].astype(F32)
    for term in terms[1:]:
        out = out + term.astype(F32)
    return out


def both_ways(pairs):
    return pairs + [(b, a) for a, b in pairs]


def before_ctx(n_ctx, own):
    odd = lax.axis_index("ctx") % 2 == 1
    before = jnp.zeros(own.shape, F32)
    if n_ctx % 2:
        for s in range(1, n_ctx):
            before = total(before, lax.ppermute(own, "ctx", [(i, i + s) for i in range(n_ctx - s)]))
        return before.astype(BF16)
    other = lax.ppermute(own, "ctx", both_ways([(i, i + 1) for i in range(0, n_ctx, 2)]))
    couple = total(own, other).astype(BF16)
    for s in range(2, n_ctx, 2):
        before = total(before, lax.ppermute(couple, "ctx", [(i, i + s) for i in range(n_ctx - s)]))
    return (before + jnp.where(odd, other.astype(F32), 0.0)).astype(BF16)


def whole_chain(n_head, own, early):
    upto = total(early, own)
    early = early.astype(F32)
    left = lax.axis_index("head") < n_head // 2
    if n_head == 1:
        return early.astype(BF16)
    if n_head % 2:
        lower = higher = jnp.zeros_like(own)
        for _ in range(n_head - 1):
            lower = lax.ppermute(
                total(lower, upto).astype(BF16), "head", [(i, i + 1) for i in range(n_head - 1)]
            )
            higher = lax.ppermute(
                total(higher, early).astype(BF16), "head", [(i + 1, i) for i in range(n_head - 1)]
            )
        return total(early, lower, higher).astype(BF16)
    mid = n_head // 2
    mine, mirror = jnp.where(left, upto, early), jnp.where(left, early, upto)
    inward = jnp.zeros_like(own)
    for t in range(mid - 1):
        inward = inward + lax.ppermute(
            total(inward, mine).astype(BF16), "head", [(t, t + 1), (n_head - 1 - t, n_head - 2 - t)]
        )
    outward = lax.ppermute(total(inward, mine).astype(BF16), "head", both_ways([(mid - 1, mid)]))
    for t in range(mid - 1, 0, -1):
        outward = outward + lax.ppermute(
            total(outward, mirror).astype(BF16), "head", [(t, t - 1), (n_head - 1 - t, n_head - t)]
        )
    return total(early, inward, outward).astype(BF16)


SKEW = 3
LATE = 2


def also(terms, *wanted):
    return [(array, first, (*had, *wanted)) for array, first, had in terms]


class Scan:
    def __init__(self, n, size):
        self.n, self.size = n, size
        self.own, self.other, self.x, self.a, self.b = {}, {}, {}, {}, {}
        self.couples = both_ways([(0, 1), (2, 3)])
        self.across = both_ways([(0, 2), (1, 3)])
        at = lambda z, c: 4 * z + c
        self.swap = both_ways(
            [(at(1, c), at(2, c)) for c in range(4)]
            + [(at(z, c), at(z, c + 1)) for z in (0, 3) for c in (0, 2)]
        )

    def begin(self, first, own):
        other = lax.ppermute(own, "ctx", self.couples)
        for i in range(own.shape[0] // self.size):
            self.own[first + i] = (own, i * self.size)
            self.other[first + i] = (other, i * self.size)

    def cross(self, c, after):
        terms = [(*self.own[c], ()), (*self.other[c], ())]
        send = combine("cross_sum", self.size, [terms], after)
        self.x[c] = (lax.ppermute(send, "ctx", self.across), 0)
        return [send]

    def early(self, c):
        return [(*self.other[c], ("odd",)), (*self.x[c], ("later",))]

    def to_right(self, c):
        if c < LATE:
            return [(*self.own[c], ()), (*self.other[c], ("odd",))]
        return [*self.early(c), (*self.own[c], ())]

    def to_left(self, c):
        if c < LATE:
            return [(*self.other[c], ()), (*self.own[c], ("even",))]
        return self.early(c)

    def mine(self, c):
        if c < LATE:
            return [*also(self.to_right(c), "left"), *also(self.to_left(c), "right")]
        return [*self.early(c), (*self.own[c], ("left",))]

    def mirror(self, c):
        if c < LATE:
            return [*also(self.to_left(c), "left"), *also(self.to_right(c), "right")]
        return [*self.early(c), (*self.own[c], ("right",))]

    def side(self, t, after):
        inwards, outwards = t < self.n, t >= SKEW
        c = t - SKEW
        terms = []
        if inwards:
            terms += also(self.mine(t), *(("outer",) if outwards else ()))
        if outwards:
            terms += also([*self.mirror(c), (*self.b[c], ())], *(("inner",) if inwards else ()))
        send = combine("side_sum", self.size, [terms], after)
        self.a[t] = (lax.ppermute(send, "head", both_ways([(0, 1), (3, 2)])), 0)
        return [send]

    def middle(self, t, after):
        send = combine("middle_sum", self.size, [[*self.mine(t), (*self.a[t], ())]], after)
        self.b[t] = (lax.ppermute(send, ("head", "ctx"), self.swap), 0)
        return [send]

    def lower(self, c):
        return [
            (*self.a[c], ("left", "inner")),
            (*self.b[c], ("right", "inner")),
            (*self.a[c + SKEW], ("right", "outer")),
        ]

    def higher(self, c):
        return [
            (*self.b[c], ("left", "inner")),
            (*self.a[c + SKEW], ("left", "outer")),
            (*self.a[c], ("right", "inner")),
        ]

    def late_cross(self, after):
        chunks = []
        for c in range(LATE):
            whole = [*self.lower(c), (*self.own[c], ()), (*self.other[c], ())]
            chunks.append([*also(self.higher(c), "even"), *also(whole, "odd")])
        send = combine("late_sum", self.size, chunks, after)
        self.late = lax.ppermute(send, "ctx", self.across)
        return [send]

    def late_swap(self, after):
        self.late = lax.optimization_barrier((self.late, *after))[0]
        self.late_other = lax.ppermute(self.late, "ctx", self.couples)

    def state(self, c):
        if c < LATE:
            at = c * self.size
            return [
                *self.lower(c),
                *also([*self.higher(c), (*self.other[c], ())], "odd"),
                (self.late, at, ("later",)),
                (self.late_other, at, ("later",)),
            ]
        return [
            *self.early(c),
            (*self.a[c], ("inner",)),
            (*self.b[c], ("inner",)),
            (*self.a[c + SKEW], ("outer",)),
        ]


def body(n_head, n_ctx, queries, keys, values, gain):
    rows, width = queries.shape[1], queries.shape[2]
    q_rows = queries.reshape(rows, width)
    k_rows = keys.reshape(rows, width)
    v_rows = values.reshape(rows, width)
    heads = width // DH
    if n_head != 4 or n_ctx != 4 or heads % 16:
        own, ka = kv_states(k_rows, v_rows, 0, heads, [])
        state = whole_chain(n_head, own, before_ctx(n_ctx, own))
        both = local_scores(q_rows, ka, 0, 0, heads, [])
        return last_attend(both, v_rows, 0, [(state, 0, ())], [], [], gain)

    n = 8
    size = heads // n
    both, attns, squares, ka = {}, {}, {}, {}
    scan = Scan(n, size)

    def kv(first, count, after, limit=VMEM_LIMIT):
        own, active = kv_states(k_rows, v_rows, first * size, count * size, after, limit)
        scan.begin(first, own)
        for i in range(count):
            ka[first + i] = (active, i * size)
        return [own]

    def scores(c, after):
        both[c] = local_scores(q_rows, *ka[c], c * size, size, after)
        return [both[c]]

    def attention(c, after):
        attns[c], squares[c] = attend(both[c], v_rows, c * size, scan.state(c), after)
        return [squares[c]]

    fill = {
        1: [0], 2: [1], 3: [2], 4: [3], 5: [4], 6: [5], 7: [6], 8: [7],
    }
    clock = kv(0, 2, [], 61 * 10**6)
    clock = kv(2, 2, clock, 60 * 10**6)
    for t in range(n + SKEW):
        clock = scan.side(t, clock)
        if t == 1:
            clock = kv(4, 4, clock)
        for c in fill.get(t, []):
            clock = scores(c, clock)
        if t > n:
            clock = attention(t - n - 1 + LATE, clock)
        if 0 <= t - 1 < n:
            clock = scan.middle(t - 1, clock)
        if t + 2 < n:
            clock = scan.cross(t + 2, clock)
        if t + 2 == n:
            clock = scan.late_cross(clock)
        if t == n + 1:
            scan.late_swap(clock)
    for c in [*range(LATE + 2, n - 2), *range(LATE), n - 2]:
        clock = attention(c, clock)
    return last_attend(
        both[n - 1], v_rows, (n - 1) * size, scan.state(n - 1),
        [attns[c] for c in range(n - 1)], [squares[c] for c in range(n - 1)], gain,
    )


def solution(mesh):
    n_head, n_ctx = mesh.shape["head"], mesh.shape["ctx"]
    return jax.shard_map(
        functools.partial(body, n_head, n_ctx),
        mesh=mesh,
        in_specs=(
            P(("rep", "ctx"), "head", None),
            P(("rep", "ctx"), "head", None),
            P(("rep", "ctx"), "head", None),
            P(),
        ),
        out_specs=P(("rep", "ctx"), "head", None),
        check_vma=False,
    )
```

```python
import functools

import jax
import jax.numpy as jnp
from jax import lax
from jax.experimental import pallas as pl
from jax.experimental.pallas import tpu as pltpu
from jax.sharding import PartitionSpec as P

DH = 128
F32 = jnp.float32
BF16 = jnp.bfloat16
VMEM_LIMIT = 8 << 20
EARLY = 10**6
COST = 2 * 10**9
VMEM = pl.BlockSpec(memory_space=pltpu.VMEM)
ANY = pl.BlockSpec(memory_space=pl.ANY)


def silu(x):
    x = x.astype(F32)
    return (x * (0.5 * jnp.tanh(0.5 * x) + 0.5)).astype(BF16)


def call(kernel, name, operands, outs, after, cost=COST):
    n_in, n_after = len(operands), len(after)

    def run(*refs):
        kernel(refs[:n_in], refs[n_in + n_after :])

    return pl.pallas_call(
        run,
        in_specs=[VMEM] * n_in + [ANY] * n_after,
        out_specs=[VMEM] * len(outs),
        out_shape=outs,
        compiler_params=pltpu.CompilerParams(vmem_limit_bytes=VMEM_LIMIT),
        cost_estimate=pl.CostEstimate(flops=cost, bytes_accessed=1, transcendentals=0),
        name=name,
    )(*operands, *after)


def head_cols(h):
    return slice(h * DH, (h + 1) * DH)


def states_of(count, rows, kind=BF16):
    return jax.ShapeDtypeStruct((count, rows, DH), kind)


def conditions():
    place, along = lax.axis_index("ctx"), lax.axis_index("head")
    outer = (along == 0) | (along == 3)
    return {
        "odd": lax.rem(place, 2) == 1,
        "even": lax.rem(place, 2) == 0,
        "later": place >= 2,
        "left": along < 2,
        "right": along >= 2,
        "outer": outer,
        "inner": jnp.logical_not(outer),
    }


def term_sum(refs, terms, held, h):
    out = None
    for ref, (_, first, wanted) in zip(refs, terms):
        x = ref[first + h].astype(F32)
        if wanted:
            x = jnp.where(held[wanted], x, 0.0)
        out = x if out is None else out + x
    return out


def combine(name, count, chunks, after, cost=COST):
    starts = [sum(len(c) for c in chunks[:i]) for i in range(len(chunks))]

    def kernel(ins, outs):
        held = Held()
        for i, terms in enumerate(chunks):
            for h in range(count):
                outs[0][i * count + h] = term_sum(ins[starts[i] :], terms, held, h).astype(BF16)

    arrays = [t[0] for terms in chunks for t in terms]
    return call(kernel, name, arrays, [states_of(count * len(chunks), DH)], after, cost)[0]


class Held:
    def __init__(self):
        self.base, self.known = conditions(), {}

    def __getitem__(self, wanted):
        if wanted not in self.known:
            out = self.base[wanted[0]]
            for name in wanted[1:]:
                out = out & self.base[name]
            self.known[wanted] = out
        return self.known[wanted]


def kv_states(k_rows, v_rows, first, count, after):
    rows = k_rows.shape[0]

    def kernel(ins, outs):
        for h in range(count):
            cols = head_cols(first + h)
            ka = silu(ins[0][:, cols])
            outs[1][:, head_cols(h)] = ka
            outs[0][h] = lax.dot_general(
                ka, ins[1][:, cols], (((0,), (0,)), ((), ())), preferred_element_type=F32
            ).astype(BF16)

    outs = [states_of(count, DH), jax.ShapeDtypeStruct((rows, count * DH), BF16)]
    return call(kernel, "kv_states", [k_rows, v_rows], outs, after, EARLY)


def local_scores(q_rows, ka, ka_first, first, count, after):
    rows = q_rows.shape[0]

    def kernel(ins, outs):
        q_ref, ka_ref = ins
        causal = lax.broadcasted_iota(jnp.int32, (rows, rows), 0) >= lax.broadcasted_iota(
            jnp.int32, (rows, rows), 1
        )
        for h in range(count):
            qa = silu(q_ref[:, head_cols(first + h)])
            scores = lax.dot_general(
                qa, ka_ref[:, head_cols(ka_first + h)], (((1,), (1,)), ((), ())),
                preferred_element_type=F32,
            )
            at = h * (rows + DH)
            outs[0][:, at : at + rows] = jnp.where(causal, scores, 0.0).astype(BF16)
            outs[0][:, at + rows : at + rows + DH] = qa

    out = jax.ShapeDtypeStruct((rows, count * (rows + DH)), BF16)
    return call(
        kernel, "local_scores", [q_rows, ka], [out], after
    )[0]


def attend_head(both_ref, v, state, h, rows):
    at = h * (rows + DH)
    right = jnp.concatenate([v, state.astype(BF16)], axis=0)
    return jnp.dot(
        both_ref[:, at : at + rows + DH], right, preferred_element_type=F32
    ).astype(BF16)


def attend(both, v_rows, first, terms, after):
    rows = both.shape[0]
    count = both.shape[1] // (rows + DH)

    def kernel(ins, outs):
        both_ref, v_ref, refs = ins[0], ins[1], ins[2:]
        held = Held()
        squares = None
        for h in range(count):
            state = term_sum(refs, terms, held, h)
            attn = attend_head(both_ref, v_ref[:, head_cols(first + h)], state, h, rows)
            outs[0][:, head_cols(h)] = attn
            wide = attn.astype(F32)
            squares = wide * wide if squares is None else squares + wide * wide
        outs[1][...] = squares

    outs = [
        jax.ShapeDtypeStruct((rows, count * DH), BF16),
        jax.ShapeDtypeStruct((rows, DH), F32),
    ]
    return call(kernel, "attend", [both, v_rows, *(t[0] for t in terms)], outs, after)


def last_attend(both, v_rows, first, terms, attns, squares, gain):
    rows, width = v_rows.shape
    count = both.shape[1] // (rows + DH)
    n_terms, n = len(terms), len(attns)
    starts = [0]
    for a in attns:
        starts.append(starts[-1] + a.shape[1])

    def kernel(*refs):
        both_ref, v_ref = refs[:2]
        term_refs = refs[2 : 2 + n_terms]
        attn_refs = refs[2 + n_terms : 2 + n_terms + n]
        sq_refs = refs[2 + n_terms + n : 2 + n_terms + 2 * n]
        gain_ref, out_hbm, done_ref, sem = refs[2 + n_terms + 2 * n :]
        held = Held()
        squares = None
        last = []
        for h in range(count):
            state = term_sum(term_refs, terms, held, h)
            attn = attend_head(both_ref, v_ref[:, head_cols(first + h)], state, h, rows)
            last.append(attn)
            wide = attn.astype(F32)
            squares = wide * wide if squares is None else squares + wide * wide
        for ref in sq_refs:
            squares = squares + ref[...]
        mean_sq = jnp.sum(squares, axis=1, keepdims=True) / width
        scale = jnp.broadcast_to(lax.rsqrt(mean_sq + 1e-06), (rows, DH))
        copies = []
        for i, start in enumerate(starts):
            wide = count * DH if i == n else attn_refs[i].shape[1]
            for h in range(wide // DH):
                cols = slice(start + h * DH, start + (h + 1) * DH)
                attn = last[h] if i == n else attn_refs[i][:, head_cols(h)]
                done_ref[:, cols] = (attn.astype(F32) * scale * gain_ref[:, cols]).astype(BF16)
            part = pl.ds(start, wide)
            copy = pltpu.make_async_copy(
                done_ref.at[:, part], out_hbm.at[0, :, part], sem.at[i]
            )
            copy.start()
            copies.append(copy)
        for copy in copies:
            copy.wait()

    operands = [both, v_rows, *(t[0] for t in terms), *attns, *squares, gain.reshape(1, width)]
    return pl.pallas_call(
        kernel,
        in_specs=[VMEM] * len(operands),
        out_specs=pl.BlockSpec(memory_space=pltpu.HBM),
        out_shape=jax.ShapeDtypeStruct((1, rows, width), BF16),
        scratch_shapes=[pltpu.VMEM((rows, width), BF16), pltpu.SemaphoreType.DMA((n + 1,))],
        compiler_params=pltpu.CompilerParams(vmem_limit_bytes=VMEM_LIMIT),
        cost_estimate=pl.CostEstimate(flops=COST, bytes_accessed=1, transcendentals=0),
        name="last_attend",
    )(*operands)


def total(*terms):
    out = terms[0].astype(F32)
    for term in terms[1:]:
        out = out + term.astype(F32)
    return out


def both_ways(pairs):
    return pairs + [(b, a) for a, b in pairs]


def before_ctx(n_ctx, own):
    odd = lax.axis_index("ctx") % 2 == 1
    before = jnp.zeros(own.shape, F32)
    if n_ctx % 2:
        for s in range(1, n_ctx):
            before = total(before, lax.ppermute(own, "ctx", [(i, i + s) for i in range(n_ctx - s)]))
        return before.astype(BF16)
    other = lax.ppermute(own, "ctx", both_ways([(i, i + 1) for i in range(0, n_ctx, 2)]))
    couple = total(own, other).astype(BF16)
    for s in range(2, n_ctx, 2):
        before = total(before, lax.ppermute(couple, "ctx", [(i, i + s) for i in range(n_ctx - s)]))
    return (before + jnp.where(odd, other.astype(F32), 0.0)).astype(BF16)


def whole_chain(n_head, own, early):
    upto = total(early, own)
    early = early.astype(F32)
    left = lax.axis_index("head") < n_head // 2
    if n_head == 1:
        return early.astype(BF16)
    if n_head % 2:
        lower = higher = jnp.zeros_like(own)
        for _ in range(n_head - 1):
            lower = lax.ppermute(
                total(lower, upto).astype(BF16), "head", [(i, i + 1) for i in range(n_head - 1)]
            )
            higher = lax.ppermute(
                total(higher, early).astype(BF16), "head", [(i + 1, i) for i in range(n_head - 1)]
            )
        return total(early, lower, higher).astype(BF16)
    mid = n_head // 2
    mine, mirror = jnp.where(left, upto, early), jnp.where(left, early, upto)
    inward = jnp.zeros_like(own)
    for t in range(mid - 1):
        inward = inward + lax.ppermute(
            total(inward, mine).astype(BF16), "head", [(t, t + 1), (n_head - 1 - t, n_head - 2 - t)]
        )
    outward = lax.ppermute(total(inward, mine).astype(BF16), "head", both_ways([(mid - 1, mid)]))
    for t in range(mid - 1, 0, -1):
        outward = outward + lax.ppermute(
            total(outward, mirror).astype(BF16), "head", [(t, t - 1), (n_head - 1 - t, n_head - t)]
        )
    return total(early, inward, outward).astype(BF16)


SKEW = 3
LATE = 2


def also(terms, *wanted):
    return [(array, first, (*had, *wanted)) for array, first, had in terms]


class Scan:
    def __init__(self, n, size):
        self.n, self.size = n, size
        self.own, self.other, self.x, self.a, self.b = {}, {}, {}, {}, {}
        self.late, self.late_other = {}, {}
        self.couples = both_ways([(0, 1), (2, 3)])
        self.across = both_ways([(0, 2), (1, 3)])
        at = lambda z, c: 4 * z + c
        self.swap = both_ways(
            [(at(1, c), at(2, c)) for c in range(4)]
            + [(at(z, c), at(z, c + 1)) for z in (0, 3) for c in (0, 2)]
        )

    def begin(self, first, own):
        other = lax.ppermute(own, "ctx", self.couples)
        for i in range(own.shape[0] // self.size):
            self.own[first + i] = (own, i * self.size)
            self.other[first + i] = (other, i * self.size)

    def cross(self, c, after):
        terms = [(*self.own[c], ()), (*self.other[c], ())]
        send = combine("cross_sum", self.size, [terms], after, EARLY if c == LATE else COST)
        self.x[c] = (lax.ppermute(send, "ctx", self.across), 0)
        return [send]

    def early(self, c):
        return [(*self.other[c], ("odd",)), (*self.x[c], ("later",))]

    def to_right(self, c):
        if c < LATE:
            return [(*self.own[c], ()), (*self.other[c], ("odd",))]
        return [*self.early(c), (*self.own[c], ())]

    def to_left(self, c):
        if c < LATE:
            return [(*self.other[c], ()), (*self.own[c], ("even",))]
        return self.early(c)

    def mine(self, c):
        if c < LATE:
            return [*also(self.to_right(c), "left"), *also(self.to_left(c), "right")]
        return [*self.early(c), (*self.own[c], ("left",))]

    def mirror(self, c):
        if c < LATE:
            return [*also(self.to_left(c), "left"), *also(self.to_right(c), "right")]
        return [*self.early(c), (*self.own[c], ("right",))]

    def side(self, t, after):
        inwards, outwards = t < self.n, t >= SKEW
        c = t - SKEW
        terms = []
        if inwards:
            terms += also(self.mine(t), *(("outer",) if outwards else ()))
        if outwards:
            terms += also([*self.mirror(c), (*self.b[c], ())], *(("inner",) if inwards else ()))
        send = combine("side_sum", self.size, [terms], after, EARLY if t == 1 else COST)
        self.a[t] = (lax.ppermute(send, "head", both_ways([(0, 1), (3, 2)])), 0)
        return [send]

    def middle(self, t, after):
        send = combine("middle_sum", self.size, [[*self.mine(t), (*self.a[t], ())]], after)
        self.b[t] = (lax.ppermute(send, ("head", "ctx"), self.swap), 0)
        return [send]

    def lower(self, c):
        return [
            (*self.a[c], ("left", "inner")),
            (*self.b[c], ("right", "inner")),
            (*self.a[c + SKEW], ("right", "outer")),
        ]

    def higher(self, c):
        return [
            (*self.b[c], ("left", "inner")),
            (*self.a[c + SKEW], ("left", "outer")),
            (*self.a[c], ("right", "inner")),
        ]

    def late_cross(self, c, after):
        whole = [*self.lower(c), (*self.own[c], ()), (*self.other[c], ())]
        terms = [*also(self.higher(c), "even"), *also(whole, "odd")]
        send = combine("late_sum", self.size, [terms], after)
        self.late[c] = lax.ppermute(send, "ctx", self.across)
        return [send]

    def late_swap(self, c, after):
        self.late[c] = lax.optimization_barrier((self.late[c], *after))[0]
        self.late_other[c] = lax.ppermute(self.late[c], "ctx", self.couples)
        return [self.late[c]]

    def state(self, c):
        if c < LATE:
            return [
                *self.lower(c),
                *also([*self.higher(c), (*self.other[c], ())], "odd"),
                (self.late[c], 0, ("later",)),
                (self.late_other[c], 0, ("later",)),
            ]
        return [
            *self.early(c),
            (*self.a[c], ("inner",)),
            (*self.b[c], ("inner",)),
            (*self.a[c + SKEW], ("outer",)),
        ]


def body(n_head, n_ctx, queries, keys, values, gain):
    rows, width = queries.shape[1], queries.shape[2]
    q_rows = queries.reshape(rows, width)
    k_rows = keys.reshape(rows, width)
    v_rows = values.reshape(rows, width)
    heads = width // DH
    if n_head != 4 or n_ctx != 4 or heads % 16:
        own, ka = kv_states(k_rows, v_rows, 0, heads, [])
        state = whole_chain(n_head, own, before_ctx(n_ctx, own))
        both = local_scores(q_rows, ka, 0, 0, heads, [])
        return last_attend(both, v_rows, 0, [(state, 0, ())], [], [], gain)

    n = 8
    size = heads // n
    both, attns, squares, ka = {}, {}, {}, {}
    scan = Scan(n, size)

    def kv(first, count, after, cut=False):
        at = first * size
        k, v = k_rows, v_rows
        if cut:
            cols = slice(at * DH, (at + count * size) * DH)
            k, v, at = k[:, cols], v[:, cols], 0
        own, active = kv_states(k, v, at, count * size, after)
        scan.begin(first, own)
        for i in range(count):
            ka[first + i] = (active, i * size)
        return [own]

    def scores(c, after):
        both[c] = local_scores(q_rows, *ka[c], c * size, size, after)
        return [both[c]]

    def attention(c, after):
        attns[c], squares[c] = attend(both[c], v_rows, c * size, scan.state(c), after)
        return [squares[c]]

    fill = {
        1: [0], 2: [1], 3: [2], 4: [3], 5: [4], 6: [5], 7: [6], 8: [7],
    }
    clock = kv(0, 1, [], cut=True)
    clock = kv(1, 1, clock, cut=True)
    clock = kv(2, 1, clock, cut=True)
    for t in range(n + SKEW):
        clock = scan.side(t, clock)
        if t == 1:
            clock = scan.cross(2, clock)
            clock = kv(3, 1, clock)
            clock = kv(4, 4, clock)
        if t == n + 1:
            clock = scan.late_swap(1, clock)
        for c in fill.get(t, []):
            clock = scores(c, clock)
        if t > n:
            clock = attention(t - n - 1 + LATE, clock)
        if 0 <= t - 1 < n:
            clock = scan.middle(t - 1, clock)
        if LATE < t + 2 < n:
            clock = scan.cross(t + 2, clock)
        if 0 <= t + 2 - n < LATE:
            clock = scan.late_cross(t + 2 - n, clock)
        if t == n:
            clock = scan.late_swap(0, clock)
    for c in [*range(LATE, n - 1), *range(LATE)]:
        if c not in attns:
            clock = attention(c, clock)
    return last_attend(
        both[n - 1], v_rows, (n - 1) * size, scan.state(n - 1),
        [attns[c] for c in range(n - 1)], [squares[c] for c in range(n - 1)], gain,
    )


def solution(mesh):
    n_head, n_ctx = mesh.shape["head"], mesh.shape["ctx"]
    return jax.shard_map(
        functools.partial(body, n_head, n_ctx),
        mesh=mesh,
        in_specs=(
            P(("rep", "ctx"), "head", None),
            P(("rep", "ctx"), "head", None),
            P(("rep", "ctx"), "head", None),
            P(),
        ),
        out_specs=P(("rep", "ctx"), "head", None),
        check_vma=False,
    )
```

```python
import functools

import jax
import jax.numpy as jnp
from jax import lax
from jax.experimental import pallas as pl
from jax.experimental.pallas import tpu as pltpu
from jax.sharding import PartitionSpec as P

DH = 128
F32 = jnp.float32
BF16 = jnp.bfloat16
VMEM_LIMIT = 8 << 20
EARLY = 10**6
COST = 2 * 10**9
VMEM = pl.BlockSpec(memory_space=pltpu.VMEM)
ANY = pl.BlockSpec(memory_space=pl.ANY)


def silu(x):
    x = x.astype(F32)
    return (x * (0.5 * jnp.tanh(0.5 * x) + 0.5)).astype(BF16)


def call(kernel, name, operands, outs, after, cost=COST):
    n_in, n_after = len(operands), len(after)

    def run(*refs):
        kernel(refs[:n_in], refs[n_in + n_after :])

    return pl.pallas_call(
        run,
        in_specs=[VMEM] * n_in + [ANY] * n_after,
        out_specs=[VMEM] * len(outs),
        out_shape=outs,
        compiler_params=pltpu.CompilerParams(vmem_limit_bytes=VMEM_LIMIT),
        cost_estimate=pl.CostEstimate(flops=cost, bytes_accessed=1, transcendentals=0),
        name=name,
    )(*operands, *after)


def head_cols(h):
    return slice(h * DH, (h + 1) * DH)


def states_of(count, rows, kind=BF16):
    return jax.ShapeDtypeStruct((count, rows, DH), kind)


def conditions():
    place, along = lax.axis_index("ctx"), lax.axis_index("head")
    outer = (along == 0) | (along == 3)
    return {
        "odd": lax.rem(place, 2) == 1,
        "even": lax.rem(place, 2) == 0,
        "later": place >= 2,
        "left": along < 2,
        "right": along >= 2,
        "outer": outer,
        "inner": jnp.logical_not(outer),
    }


def term_sum(refs, terms, held, h):
    out = None
    for ref, (_, first, wanted) in zip(refs, terms):
        x = ref[first + h].astype(F32)
        if wanted:
            x = jnp.where(held[wanted], x, 0.0)
        out = x if out is None else out + x
    return out


def combine(name, count, chunks, after, cost=COST):
    starts = [sum(len(c) for c in chunks[:i]) for i in range(len(chunks))]

    def kernel(ins, outs):
        held = Held()
        for i, terms in enumerate(chunks):
            for h in range(count):
                outs[0][i * count + h] = term_sum(ins[starts[i] :], terms, held, h).astype(BF16)

    arrays = [t[0] for terms in chunks for t in terms]
    return call(kernel, name, arrays, [states_of(count * len(chunks), DH)], after, cost)[0]


class Held:
    def __init__(self):
        self.base, self.known = conditions(), {}

    def __getitem__(self, wanted):
        if wanted not in self.known:
            out = self.base[wanted[0]]
            for name in wanted[1:]:
                out = out & self.base[name]
            self.known[wanted] = out
        return self.known[wanted]


def kv_states(k_rows, v_rows, first, count, after):
    rows = k_rows.shape[0]

    def kernel(ins, outs):
        for h in range(count):
            cols = head_cols(first + h)
            ka = silu(ins[0][:, cols])
            outs[1][:, head_cols(h)] = ka
            outs[0][h] = lax.dot_general(
                ka, ins[1][:, cols], (((0,), (0,)), ((), ())), preferred_element_type=F32
            ).astype(BF16)

    outs = [states_of(count, DH), jax.ShapeDtypeStruct((rows, count * DH), BF16)]
    return call(kernel, "kv_states", [k_rows, v_rows], outs, after, EARLY)


def local_scores(q_rows, ka, ka_first, first, count, after):
    rows = q_rows.shape[0]

    def kernel(ins, outs):
        q_ref, ka_ref = ins
        causal = lax.broadcasted_iota(jnp.int32, (rows, rows), 0) >= lax.broadcasted_iota(
            jnp.int32, (rows, rows), 1
        )
        for h in range(count):
            qa = silu(q_ref[:, head_cols(first + h)])
            scores = lax.dot_general(
                qa, ka_ref[:, head_cols(ka_first + h)], (((1,), (1,)), ((), ())),
                preferred_element_type=F32,
            )
            at = h * (rows + DH)
            outs[0][:, at : at + rows] = jnp.where(causal, scores, 0.0).astype(BF16)
            outs[0][:, at + rows : at + rows + DH] = qa

    out = jax.ShapeDtypeStruct((rows, count * (rows + DH)), BF16)
    return call(
        kernel, "local_scores", [q_rows, ka], [out], after
    )[0]


def attend_head(both_ref, v, state, h, rows):
    at = h * (rows + DH)
    right = jnp.concatenate([v, state.astype(BF16)], axis=0)
    return jnp.dot(
        both_ref[:, at : at + rows + DH], right, preferred_element_type=F32
    ).astype(BF16)


def attend(both, v_rows, first, terms, after):
    rows = both.shape[0]
    count = both.shape[1] // (rows + DH)

    def kernel(ins, outs):
        both_ref, v_ref, refs = ins[0], ins[1], ins[2:]
        held = Held()
        squares = None
        for h in range(count):
            state = term_sum(refs, terms, held, h)
            attn = attend_head(both_ref, v_ref[:, head_cols(first + h)], state, h, rows)
            outs[0][:, head_cols(h)] = attn
            wide = attn.astype(F32)
            squares = wide * wide if squares is None else squares + wide * wide
        outs[1][...] = squares

    outs = [
        jax.ShapeDtypeStruct((rows, count * DH), BF16),
        jax.ShapeDtypeStruct((rows, DH), F32),
    ]
    return call(kernel, "attend", [both, v_rows, *(t[0] for t in terms)], outs, after)


def last_attend(both, v_rows, first, terms, attns, squares, gain):
    rows, width = v_rows.shape
    count = both.shape[1] // (rows + DH)
    n_terms, n = len(terms), len(attns)
    starts = [0]
    for a in attns:
        starts.append(starts[-1] + a.shape[1])

    def kernel(*refs):
        both_ref, v_ref = refs[:2]
        term_refs = refs[2 : 2 + n_terms]
        attn_refs = refs[2 + n_terms : 2 + n_terms + n]
        sq_refs = refs[2 + n_terms + n : 2 + n_terms + 2 * n]
        gain_ref, out_hbm, done_ref, sem = refs[2 + n_terms + 2 * n :]
        held = Held()
        squares = None
        last = []
        for h in range(count):
            state = term_sum(term_refs, terms, held, h)
            attn = attend_head(both_ref, v_ref[:, head_cols(first + h)], state, h, rows)
            last.append(attn)
            wide = attn.astype(F32)
            squares = wide * wide if squares is None else squares + wide * wide
        for ref in sq_refs:
            squares = squares + ref[...]
        mean_sq = jnp.sum(squares, axis=1, keepdims=True) / width
        scale = jnp.broadcast_to(lax.rsqrt(mean_sq + 1e-06), (rows, DH))
        copies = []
        for i, start in enumerate(starts):
            wide = count * DH if i == n else attn_refs[i].shape[1]
            for h in range(wide // DH):
                cols = slice(start + h * DH, start + (h + 1) * DH)
                attn = last[h] if i == n else attn_refs[i][:, head_cols(h)]
                done_ref[:, cols] = (attn.astype(F32) * scale * gain_ref[:, cols]).astype(BF16)
            part = pl.ds(start, wide)
            copy = pltpu.make_async_copy(
                done_ref.at[:, part], out_hbm.at[0, :, part], sem.at[i]
            )
            copy.start()
            copies.append(copy)
        for copy in copies:
            copy.wait()

    operands = [both, v_rows, *(t[0] for t in terms), *attns, *squares, gain.reshape(1, width)]
    return pl.pallas_call(
        kernel,
        in_specs=[VMEM] * len(operands),
        out_specs=pl.BlockSpec(memory_space=pltpu.HBM),
        out_shape=jax.ShapeDtypeStruct((1, rows, width), BF16),
        scratch_shapes=[pltpu.VMEM((rows, width), BF16), pltpu.SemaphoreType.DMA((n + 1,))],
        compiler_params=pltpu.CompilerParams(vmem_limit_bytes=VMEM_LIMIT),
        cost_estimate=pl.CostEstimate(flops=COST, bytes_accessed=1, transcendentals=0),
        name="last_attend",
    )(*operands)


def total(*terms):
    out = terms[0].astype(F32)
    for term in terms[1:]:
        out = out + term.astype(F32)
    return out


def both_ways(pairs):
    return pairs + [(b, a) for a, b in pairs]


def before_ctx(n_ctx, own):
    odd = lax.axis_index("ctx") % 2 == 1
    before = jnp.zeros(own.shape, F32)
    if n_ctx % 2:
        for s in range(1, n_ctx):
            before = total(before, lax.ppermute(own, "ctx", [(i, i + s) for i in range(n_ctx - s)]))
        return before.astype(BF16)
    other = lax.ppermute(own, "ctx", both_ways([(i, i + 1) for i in range(0, n_ctx, 2)]))
    couple = total(own, other).astype(BF16)
    for s in range(2, n_ctx, 2):
        before = total(before, lax.ppermute(couple, "ctx", [(i, i + s) for i in range(n_ctx - s)]))
    return (before + jnp.where(odd, other.astype(F32), 0.0)).astype(BF16)


def whole_chain(n_head, own, early):
    upto = total(early, own)
    early = early.astype(F32)
    left = lax.axis_index("head") < n_head // 2
    if n_head == 1:
        return early.astype(BF16)
    if n_head % 2:
        lower = higher = jnp.zeros_like(own)
        for _ in range(n_head - 1):
            lower = lax.ppermute(
                total(lower, upto).astype(BF16), "head", [(i, i + 1) for i in range(n_head - 1)]
            )
            higher = lax.ppermute(
                total(higher, early).astype(BF16), "head", [(i + 1, i) for i in range(n_head - 1)]
            )
        return total(early, lower, higher).astype(BF16)
    mid = n_head // 2
    mine, mirror = jnp.where(left, upto, early), jnp.where(left, early, upto)
    inward = jnp.zeros_like(own)
    for t in range(mid - 1):
        inward = inward + lax.ppermute(
            total(inward, mine).astype(BF16), "head", [(t, t + 1), (n_head - 1 - t, n_head - 2 - t)]
        )
    outward = lax.ppermute(total(inward, mine).astype(BF16), "head", both_ways([(mid - 1, mid)]))
    for t in range(mid - 1, 0, -1):
        outward = outward + lax.ppermute(
            total(outward, mirror).astype(BF16), "head", [(t, t - 1), (n_head - 1 - t, n_head - t)]
        )
    return total(early, inward, outward).astype(BF16)


SKEW = 3
LATE = 2


def also(terms, *wanted):
    return [(array, first, (*had, *wanted)) for array, first, had in terms]


class Scan:
    def __init__(self, n, size):
        self.n, self.size = n, size
        self.own, self.other, self.x, self.a, self.b = {}, {}, {}, {}, {}
        self.late, self.late_other, self.whole = {}, {}, {}
        self.couples = both_ways([(0, 1), (2, 3)])
        self.across = both_ways([(0, 2), (1, 3)])
        at = lambda z, c: 4 * z + c
        self.swap = both_ways(
            [(at(1, c), at(2, c)) for c in range(4)]
            + [(at(z, c), at(z, c + 1)) for z in (0, 3) for c in (0, 2)]
        )

    def begin(self, first, own):
        if first < LATE:
            self.own[first] = (own, 0)
            return
        other = lax.ppermute(own, "ctx", self.couples)
        for i in range(own.shape[0] // self.size):
            self.own[first + i] = (own, i * self.size)
            self.other[first + i] = (other, i * self.size)

    def cross(self, c, after):
        terms = [(*self.own[c], ()), (*self.other[c], ())]
        send = combine("cross_sum", self.size, [terms], after, EARLY if c == LATE else COST)
        self.x[c] = (lax.ppermute(send, "ctx", self.across), 0)
        return [send]

    def early(self, c):
        return [(*self.other[c], ("odd",)), (*self.x[c], ("later",))]

    def mine(self, c):
        if c < LATE:
            return [(*self.own[c], ())]
        return [*self.early(c), (*self.own[c], ("left",))]

    def mirror(self, c):
        if c < LATE:
            return [(*self.own[c], ())]
        return [*self.early(c), (*self.own[c], ("right",))]

    def side(self, t, after):
        inwards, outwards = t < self.n, t >= SKEW
        c = t - SKEW
        terms = []
        if inwards:
            terms += also(self.mine(t), *(("outer",) if outwards else ()))
        if outwards:
            terms += also([*self.mirror(c), (*self.b[c], ())], *(("inner",) if inwards else ()))
        send = combine("side_sum", self.size, [terms], after, EARLY if t == 1 else COST)
        self.a[t] = (lax.ppermute(send, "head", both_ways([(0, 1), (3, 2)])), 0)
        return [send]

    def middle(self, t, after):
        send = combine("middle_sum", self.size, [[*self.mine(t), (*self.a[t], ())]], after)
        self.b[t] = (lax.ppermute(send, ("head", "ctx"), self.swap), 0)
        return [send]

    def lower(self, c):
        return [
            (*self.a[c], ("left", "inner")),
            (*self.b[c], ("right", "inner")),
            (*self.a[c + SKEW], ("right", "outer")),
        ]

    def higher(self, c):
        return [
            (*self.b[c], ("left", "inner")),
            (*self.a[c + SKEW], ("left", "outer")),
            (*self.a[c], ("right", "inner")),
        ]

    def late_cross(self, c, after):
        terms = [*self.lower(c), (*self.own[c], ()), *self.higher(c)]
        send = combine("late_sum", self.size, [terms], after, EARLY)
        self.whole[c] = (send, 0)
        self.late[c] = (lax.ppermute(send, "ctx", self.across), 0)
        return [send]

    def late_swap(self, c, after):
        terms = [(*self.late[c], ("later",)), (*self.whole[c], ("even",))]
        send = combine("late_swap", self.size, [terms], after, EARLY)
        self.late_other[c] = (lax.ppermute(send, "ctx", self.couples), 0)
        return [send]

    def state(self, c):
        if c < LATE:
            return [*self.lower(c), (*self.late[c], ("later",)), (*self.late_other[c], ())]
        return [
            *self.early(c),
            (*self.a[c], ("inner",)),
            (*self.b[c], ("inner",)),
            (*self.a[c + SKEW], ("outer",)),
        ]


def body(n_head, n_ctx, queries, keys, values, gain):
    rows, width = queries.shape[1], queries.shape[2]
    q_rows = queries.reshape(rows, width)
    k_rows = keys.reshape(rows, width)
    v_rows = values.reshape(rows, width)
    heads = width // DH
    if n_head != 4 or n_ctx != 4 or heads % 16:
        own, ka = kv_states(k_rows, v_rows, 0, heads, [])
        state = whole_chain(n_head, own, before_ctx(n_ctx, own))
        both = local_scores(q_rows, ka, 0, 0, heads, [])
        return last_attend(both, v_rows, 0, [(state, 0, ())], [], [], gain)

    n = 8
    size = heads // n
    both, attns, squares, ka = {}, {}, {}, {}
    scan = Scan(n, size)

    def kv(first, count, after, cut=False):
        at = first * size
        k, v = k_rows, v_rows
        if cut:
            cols = slice(at * DH, (at + count * size) * DH)
            k, v, at = k[:, cols], v[:, cols], 0
        own, active = kv_states(k, v, at, count * size, after)
        scan.begin(first, own)
        for i in range(count):
            ka[first + i] = (active, i * size)
        return [own]

    def scores(c, after):
        both[c] = local_scores(q_rows, *ka[c], c * size, size, after)
        return [both[c]]

    def attention(c, after):
        attns[c], squares[c] = attend(both[c], v_rows, c * size, scan.state(c), after)
        return [squares[c]]

    fill = {
        1: [0], 2: [1], 3: [2], 4: [3], 5: [4], 6: [5], 7: [6], 8: [7],
    }
    clock = kv(2, 1, [], cut=True)
    clock = kv(0, 1, clock, cut=True)
    for t in range(n + SKEW):
        clock = scan.side(t, clock)
        if t == 0:
            clock = kv(1, 1, clock, cut=True)
        if t == 1:
            clock = scan.cross(2, clock)
            clock = kv(3, 1, clock)
            clock = kv(4, 4, clock)
        if t == n + 1:
            clock = scan.late_swap(1, clock)
        for c in fill.get(t, []):
            clock = scores(c, clock)
        if t > n:
            clock = attention(t - n - 1 + LATE, clock)
        if 0 <= t - 1 < n:
            clock = scan.middle(t - 1, clock)
        if LATE < t + 2 < n:
            clock = scan.cross(t + 2, clock)
        if 0 <= t + 2 - n < LATE:
            clock = scan.late_cross(t + 2 - n, clock)
        if t == n:
            clock = scan.late_swap(0, clock)
    for c in [*range(LATE, n - 1), *range(LATE)]:
        if c not in attns:
            clock = attention(c, clock)
    return last_attend(
        both[n - 1], v_rows, (n - 1) * size, scan.state(n - 1),
        [attns[c] for c in range(n - 1)], [squares[c] for c in range(n - 1)], gain,
    )


def solution(mesh):
    n_head, n_ctx = mesh.shape["head"], mesh.shape["ctx"]
    return jax.shard_map(
        functools.partial(body, n_head, n_ctx),
        mesh=mesh,
        in_specs=(
            P(("rep", "ctx"), "head", None),
            P(("rep", "ctx"), "head", None),
            P(("rep", "ctx"), "head", None),
            P(),
        ),
        out_specs=P(("rep", "ctx"), "head", None),
        check_vma=False,
    )
```

```python
import functools

import jax
import jax.numpy as jnp
from jax import lax
from jax.experimental import pallas as pl
from jax.experimental.pallas import tpu as pltpu
from jax.sharding import PartitionSpec as P

DH = 128
F32 = jnp.float32
BF16 = jnp.bfloat16
VMEM_LIMIT = 8 << 20
EARLY = 10**6
COST = 3 * 10**9
VMEM = pl.BlockSpec(memory_space=pltpu.VMEM)
ANY = pl.BlockSpec(memory_space=pl.ANY)


def silu(x):
    x = x.astype(F32)
    return (x * (0.5 * jnp.tanh(0.5 * x) + 0.5)).astype(BF16)


def call(kernel, name, operands, outs, after, cost=COST):
    n_in, n_after = len(operands), len(after)

    def run(*refs):
        kernel(refs[:n_in], refs[n_in + n_after :])

    return pl.pallas_call(
        run,
        in_specs=[VMEM] * n_in + [ANY] * n_after,
        out_specs=[VMEM] * len(outs),
        out_shape=outs,
        compiler_params=pltpu.CompilerParams(vmem_limit_bytes=VMEM_LIMIT),
        cost_estimate=pl.CostEstimate(flops=cost, bytes_accessed=1, transcendentals=0),
        name=name,
    )(*operands, *after)


def head_cols(h):
    return slice(h * DH, (h + 1) * DH)


def states_of(count, rows, kind=BF16):
    return jax.ShapeDtypeStruct((count, rows, DH), kind)


def conditions():
    place, along = lax.axis_index("ctx"), lax.axis_index("head")
    outer = (along == 0) | (along == 3)
    return {
        "odd": lax.rem(place, 2) == 1,
        "even": lax.rem(place, 2) == 0,
        "later": place >= 2,
        "left": along < 2,
        "right": along >= 2,
        "outer": outer,
        "inner": jnp.logical_not(outer),
    }


def term_sum(refs, terms, held, h):
    out = None
    for ref, (_, first, wanted) in zip(refs, terms):
        x = ref[first + h].astype(F32)
        if wanted:
            x = jnp.where(held[wanted], x, 0.0)
        out = x if out is None else out + x
    return out


def combine(name, count, chunks, after, cost=COST):
    starts = [sum(len(c) for c in chunks[:i]) for i in range(len(chunks))]

    def kernel(ins, outs):
        held = Held()
        for i, terms in enumerate(chunks):
            for h in range(count):
                outs[0][i * count + h] = term_sum(ins[starts[i] :], terms, held, h).astype(BF16)

    arrays = [t[0] for terms in chunks for t in terms]
    return call(kernel, name, arrays, [states_of(count * len(chunks), DH)], after, cost)[0]


class Held:
    def __init__(self):
        self.base, self.known = conditions(), {}

    def __getitem__(self, wanted):
        if wanted not in self.known:
            out = self.base[wanted[0]]
            for name in wanted[1:]:
                out = out & self.base[name]
            self.known[wanted] = out
        return self.known[wanted]


def kv_states(k_rows, v_rows, first, count, after):
    rows = k_rows.shape[0]

    def kernel(ins, outs):
        for h in range(count):
            cols = head_cols(first + h)
            ka = silu(ins[0][:, cols])
            outs[1][:, head_cols(h)] = ka
            outs[0][h] = lax.dot_general(
                ka, ins[1][:, cols], (((0,), (0,)), ((), ())), preferred_element_type=F32
            ).astype(BF16)

    outs = [states_of(count, DH), jax.ShapeDtypeStruct((rows, count * DH), BF16)]
    return call(kernel, "kv_states", [k_rows, v_rows], outs, after, EARLY)


def local_scores(q_rows, ka, ka_first, first, count, after):
    rows = q_rows.shape[0]

    def kernel(ins, outs):
        q_ref, ka_ref = ins
        causal = lax.broadcasted_iota(jnp.int32, (rows, rows), 0) >= lax.broadcasted_iota(
            jnp.int32, (rows, rows), 1
        )
        for h in range(count):
            qa = silu(q_ref[:, head_cols(first + h)])
            scores = lax.dot_general(
                qa, ka_ref[:, head_cols(ka_first + h)], (((1,), (1,)), ((), ())),
                preferred_element_type=F32,
            )
            at = h * (rows + DH)
            outs[0][:, at : at + rows] = jnp.where(causal, scores, 0.0).astype(BF16)
            outs[0][:, at + rows : at + rows + DH] = qa

    out = jax.ShapeDtypeStruct((rows, count * (rows + DH)), BF16)
    return call(
        kernel, "local_scores", [q_rows, ka], [out], after
    )[0]


def attend_head(both_ref, v, state, h, rows):
    at = h * (rows + DH)
    right = jnp.concatenate([v, state.astype(BF16)], axis=0)
    return jnp.dot(
        both_ref[:, at : at + rows + DH], right, preferred_element_type=F32
    ).astype(BF16)


def attend(both, v_rows, first, terms, after):
    rows = both.shape[0]
    count = both.shape[1] // (rows + DH)

    def kernel(ins, outs):
        both_ref, v_ref, refs = ins[0], ins[1], ins[2:]
        held = Held()
        squares = None
        for h in range(count):
            state = term_sum(refs, terms, held, h)
            attn = attend_head(both_ref, v_ref[:, head_cols(first + h)], state, h, rows)
            outs[0][:, head_cols(h)] = attn
            wide = attn.astype(F32)
            squares = wide * wide if squares is None else squares + wide * wide
        outs[1][...] = squares

    outs = [
        jax.ShapeDtypeStruct((rows, count * DH), BF16),
        jax.ShapeDtypeStruct((rows, DH), F32),
    ]
    return call(kernel, "attend", [both, v_rows, *(t[0] for t in terms)], outs, after)


def last_attend(both, v_rows, first, terms, attns, squares, gain):
    rows, width = v_rows.shape
    count = both.shape[1] // (rows + DH)
    n_terms, n = len(terms), len(attns)
    starts = [0]
    for a in attns:
        starts.append(starts[-1] + a.shape[1])

    def kernel(*refs):
        both_ref, v_ref = refs[:2]
        term_refs = refs[2 : 2 + n_terms]
        attn_refs = refs[2 + n_terms : 2 + n_terms + n]
        sq_refs = refs[2 + n_terms + n : 2 + n_terms + 2 * n]
        gain_ref, out_hbm, done_ref, sem = refs[2 + n_terms + 2 * n :]
        held = Held()
        squares = None
        last = []
        for h in range(count):
            state = term_sum(term_refs, terms, held, h)
            attn = attend_head(both_ref, v_ref[:, head_cols(first + h)], state, h, rows)
            last.append(attn)
            wide = attn.astype(F32)
            squares = wide * wide if squares is None else squares + wide * wide
        for ref in sq_refs:
            squares = squares + ref[...]
        mean_sq = jnp.sum(squares, axis=1, keepdims=True) / width
        scale = jnp.broadcast_to(lax.rsqrt(mean_sq + 1e-06), (rows, DH))
        copies = []
        for i, start in enumerate(starts):
            wide = count * DH if i == n else attn_refs[i].shape[1]
            for h in range(wide // DH):
                cols = slice(start + h * DH, start + (h + 1) * DH)
                attn = last[h] if i == n else attn_refs[i][:, head_cols(h)]
                done_ref[:, cols] = (attn.astype(F32) * scale * gain_ref[:, cols]).astype(BF16)
            part = pl.ds(start, wide)
            copy = pltpu.make_async_copy(
                done_ref.at[:, part], out_hbm.at[0, :, part], sem.at[i]
            )
            copy.start()
            copies.append(copy)
        for copy in copies:
            copy.wait()

    operands = [both, v_rows, *(t[0] for t in terms), *attns, *squares, gain.reshape(1, width)]
    return pl.pallas_call(
        kernel,
        in_specs=[VMEM] * len(operands),
        out_specs=pl.BlockSpec(memory_space=pltpu.HBM),
        out_shape=jax.ShapeDtypeStruct((1, rows, width), BF16),
        scratch_shapes=[pltpu.VMEM((rows, width), BF16), pltpu.SemaphoreType.DMA((n + 1,))],
        compiler_params=pltpu.CompilerParams(vmem_limit_bytes=VMEM_LIMIT),
        cost_estimate=pl.CostEstimate(flops=COST, bytes_accessed=1, transcendentals=0),
        name="last_attend",
    )(*operands)


def total(*terms):
    out = terms[0].astype(F32)
    for term in terms[1:]:
        out = out + term.astype(F32)
    return out


def both_ways(pairs):
    return pairs + [(b, a) for a, b in pairs]


def before_ctx(n_ctx, own):
    odd = lax.axis_index("ctx") % 2 == 1
    before = jnp.zeros(own.shape, F32)
    if n_ctx % 2:
        for s in range(1, n_ctx):
            before = total(before, lax.ppermute(own, "ctx", [(i, i + s) for i in range(n_ctx - s)]))
        return before.astype(BF16)
    other = lax.ppermute(own, "ctx", both_ways([(i, i + 1) for i in range(0, n_ctx, 2)]))
    couple = total(own, other).astype(BF16)
    for s in range(2, n_ctx, 2):
        before = total(before, lax.ppermute(couple, "ctx", [(i, i + s) for i in range(n_ctx - s)]))
    return (before + jnp.where(odd, other.astype(F32), 0.0)).astype(BF16)


def whole_chain(n_head, own, early):
    upto = total(early, own)
    early = early.astype(F32)
    left = lax.axis_index("head") < n_head // 2
    if n_head == 1:
        return early.astype(BF16)
    if n_head % 2:
        lower = higher = jnp.zeros_like(own)
        for _ in range(n_head - 1):
            lower = lax.ppermute(
                total(lower, upto).astype(BF16), "head", [(i, i + 1) for i in range(n_head - 1)]
            )
            higher = lax.ppermute(
                total(higher, early).astype(BF16), "head", [(i + 1, i) for i in range(n_head - 1)]
            )
        return total(early, lower, higher).astype(BF16)
    mid = n_head // 2
    mine, mirror = jnp.where(left, upto, early), jnp.where(left, early, upto)
    inward = jnp.zeros_like(own)
    for t in range(mid - 1):
        inward = inward + lax.ppermute(
            total(inward, mine).astype(BF16), "head", [(t, t + 1), (n_head - 1 - t, n_head - 2 - t)]
        )
    outward = lax.ppermute(total(inward, mine).astype(BF16), "head", both_ways([(mid - 1, mid)]))
    for t in range(mid - 1, 0, -1):
        outward = outward + lax.ppermute(
            total(outward, mirror).astype(BF16), "head", [(t, t - 1), (n_head - 1 - t, n_head - t)]
        )
    return total(early, inward, outward).astype(BF16)


SKEW = 3
LATE = 2


def also(terms, *wanted):
    return [(array, first, (*had, *wanted)) for array, first, had in terms]


class Scan:
    def __init__(self, n, size):
        self.n, self.size = n, size
        self.own, self.other, self.x, self.a, self.b = {}, {}, {}, {}, {}
        self.late, self.late_other, self.whole = {}, {}, {}
        self.couples = both_ways([(0, 1), (2, 3)])
        self.across = both_ways([(0, 2), (1, 3)])
        at = lambda z, c: 4 * z + c
        self.swap = both_ways(
            [(at(1, c), at(2, c)) for c in range(4)]
            + [(at(z, c), at(z, c + 1)) for z in (0, 3) for c in (0, 2)]
        )

    def begin(self, first, own):
        if first < LATE:
            self.own[first] = (own, 0)
            return
        other = lax.ppermute(own, "ctx", self.couples)
        for i in range(own.shape[0] // self.size):
            self.own[first + i] = (own, i * self.size)
            self.other[first + i] = (other, i * self.size)

    def cross(self, c, after):
        terms = [(*self.own[c], ()), (*self.other[c], ())]
        send = combine("cross_sum", self.size, [terms], after, EARLY if c == LATE else COST)
        self.x[c] = (lax.ppermute(send, "ctx", self.across), 0)
        return [send]

    def early(self, c):
        return [(*self.other[c], ("odd",)), (*self.x[c], ("later",))]

    def mine(self, c):
        if c < LATE:
            return [(*self.own[c], ())]
        return [*self.early(c), (*self.own[c], ("left",))]

    def mirror(self, c):
        if c < LATE:
            return [(*self.own[c], ())]
        return [*self.early(c), (*self.own[c], ("right",))]

    def side(self, t, after):
        inwards, outwards = t < self.n, t >= SKEW
        c = t - SKEW
        terms = []
        if inwards:
            terms += also(self.mine(t), *(("outer",) if outwards else ()))
        if outwards:
            terms += also([*self.mirror(c), (*self.b[c], ())], *(("inner",) if inwards else ()))
        send = combine("side_sum", self.size, [terms], after, EARLY if t == 1 else COST)
        self.a[t] = (lax.ppermute(send, "head", both_ways([(0, 1), (3, 2)])), 0)
        return [send]

    def middle(self, t, after):
        send = combine("middle_sum", self.size, [[*self.mine(t), (*self.a[t], ())]], after)
        self.b[t] = (lax.ppermute(send, ("head", "ctx"), self.swap), 0)
        return [send]

    def lower(self, c):
        return [
            (*self.a[c], ("left", "inner")),
            (*self.b[c], ("right", "inner")),
            (*self.a[c + SKEW], ("right", "outer")),
        ]

    def higher(self, c):
        return [
            (*self.b[c], ("left", "inner")),
            (*self.a[c + SKEW], ("left", "outer")),
            (*self.a[c], ("right", "inner")),
        ]

    def late_cross(self, c, after):
        terms = [*self.lower(c), (*self.own[c], ()), *self.higher(c)]
        send = combine("late_sum", self.size, [terms], after, EARLY)
        self.whole[c] = (send, 0)
        self.late[c] = (lax.ppermute(send, "ctx", self.across), 0)
        return [send]

    def late_swap(self, c, after):
        terms = [(*self.late[c], ("later",)), (*self.whole[c], ("even",))]
        send = combine("late_swap", self.size, [terms], after, EARLY)
        self.late_other[c] = (lax.ppermute(send, "ctx", self.couples), 0)
        return [send]

    def state(self, c):
        if c < LATE:
            return [*self.lower(c), (*self.late[c], ("later",)), (*self.late_other[c], ())]
        return [
            *self.early(c),
            (*self.a[c], ("inner",)),
            (*self.b[c], ("inner",)),
            (*self.a[c + SKEW], ("outer",)),
        ]


def body(n_head, n_ctx, queries, keys, values, gain):
    rows, width = queries.shape[1], queries.shape[2]
    q_rows = queries.reshape(rows, width)
    k_rows = keys.reshape(rows, width)
    v_rows = values.reshape(rows, width)
    heads = width // DH
    if n_head != 4 or n_ctx != 4 or heads % 16:
        own, ka = kv_states(k_rows, v_rows, 0, heads, [])
        state = whole_chain(n_head, own, before_ctx(n_ctx, own))
        both = local_scores(q_rows, ka, 0, 0, heads, [])
        return last_attend(both, v_rows, 0, [(state, 0, ())], [], [], gain)

    n = 8
    size = heads // n
    both, attns, squares, ka = {}, {}, {}, {}
    scan = Scan(n, size)

    def kv(first, count, after, cut=False):
        at = first * size
        k, v = k_rows, v_rows
        if cut:
            cols = slice(at * DH, (at + count * size) * DH)
            k, v, at = k[:, cols], v[:, cols], 0
        own, active = kv_states(k, v, at, count * size, after)
        scan.begin(first, own)
        for i in range(count):
            ka[first + i] = (active, i * size)
        return [own]

    def scores(c, after):
        both[c] = local_scores(q_rows, *ka[c], c * size, size, after)
        return [both[c]]

    def attention(c, after):
        attns[c], squares[c] = attend(both[c], v_rows, c * size, scan.state(c), after)
        return [squares[c]]

    fill = {
        1: [0], 2: [1], 3: [2], 4: [3], 5: [4], 6: [5], 7: [6], 8: [7],
    }
    clock = kv(2, 1, [], cut=True)
    clock = kv(0, 1, clock, cut=True)
    for t in range(n + SKEW):
        clock = scan.side(t, clock)
        if t == 0:
            clock = kv(1, 1, clock, cut=True)
        if t == 1:
            clock = scan.cross(2, clock)
            clock = kv(3, 1, clock)
            clock = kv(4, 4, clock)
        if t == n + 1:
            clock = scan.late_swap(0, clock)
        if t == n + 2:
            clock = scan.late_swap(1, clock)
        for c in fill.get(t, []):
            clock = scores(c, clock)
        if t > n:
            clock = attention(t - n - 1 + LATE, clock)
        if 0 <= t - 1 < n:
            clock = scan.middle(t - 1, clock)
        if LATE < t + 2 < n:
            clock = scan.cross(t + 2, clock)
        if 0 <= t + 2 - n < LATE:
            clock = scan.late_cross(t + 2 - n, clock)
    for c in [*range(LATE, n - 1), *range(LATE)]:
        if c not in attns:
            clock = attention(c, clock)
    return last_attend(
        both[n - 1], v_rows, (n - 1) * size, scan.state(n - 1),
        [attns[c] for c in range(n - 1)], [squares[c] for c in range(n - 1)], gain,
    )


def solution(mesh):
    n_head, n_ctx = mesh.shape["head"], mesh.shape["ctx"]
    return jax.shard_map(
        functools.partial(body, n_head, n_ctx),
        mesh=mesh,
        in_specs=(
            P(("rep", "ctx"), "head", None),
            P(("rep", "ctx"), "head", None),
            P(("rep", "ctx"), "head", None),
            P(),
        ),
        out_specs=P(("rep", "ctx"), "head", None),
        check_vma=False,
    )
```

```python
import functools

import jax
import jax.numpy as jnp
from jax import lax
from jax.experimental import pallas as pl
from jax.experimental.pallas import tpu as pltpu
from jax.sharding import PartitionSpec as P

DH = 128
F32 = jnp.float32
BF16 = jnp.bfloat16
VMEM_LIMIT = 8 << 20
EARLY = 10**6
COST = 3 * 10**9
VMEM = pl.BlockSpec(memory_space=pltpu.VMEM)
ANY = pl.BlockSpec(memory_space=pl.ANY)


def silu(x):
    x = x.astype(F32)
    return (x * (0.5 * jnp.tanh(0.5 * x) + 0.5)).astype(BF16)


def call(kernel, name, operands, outs, after, cost=COST):
    n_in, n_after = len(operands), len(after)

    def run(*refs):
        kernel(refs[:n_in], refs[n_in + n_after :])

    return pl.pallas_call(
        run,
        in_specs=[VMEM] * n_in + [ANY] * n_after,
        out_specs=[VMEM] * len(outs),
        out_shape=outs,
        compiler_params=pltpu.CompilerParams(vmem_limit_bytes=VMEM_LIMIT),
        cost_estimate=pl.CostEstimate(flops=cost, bytes_accessed=1, transcendentals=0),
        name=name,
    )(*operands, *after)


def head_cols(h):
    return slice(h * DH, (h + 1) * DH)


def states_of(count, rows, kind=BF16):
    return jax.ShapeDtypeStruct((count, rows, DH), kind)


def conditions():
    place, along = lax.axis_index("ctx"), lax.axis_index("head")
    outer = (along == 0) | (along == 3)
    return {
        "odd": lax.rem(place, 2) == 1,
        "even": lax.rem(place, 2) == 0,
        "later": place >= 2,
        "left": along < 2,
        "right": along >= 2,
        "outer": outer,
        "inner": jnp.logical_not(outer),
    }


def term_sum(refs, terms, held, h):
    out = None
    for ref, (_, first, wanted) in zip(refs, terms):
        x = ref[first + h].astype(F32)
        if wanted:
            x = jnp.where(held[wanted], x, 0.0)
        out = x if out is None else out + x
    return out


def combine(name, count, chunks, after, cost=COST):
    starts = [sum(len(c) for c in chunks[:i]) for i in range(len(chunks))]

    def kernel(ins, outs):
        held = Held()
        for i, terms in enumerate(chunks):
            for h in range(count):
                outs[0][i * count + h] = term_sum(ins[starts[i] :], terms, held, h).astype(BF16)

    arrays = [t[0] for terms in chunks for t in terms]
    return call(kernel, name, arrays, [states_of(count * len(chunks), DH)], after, cost)[0]


class Held:
    def __init__(self):
        self.base, self.known = conditions(), {}

    def __getitem__(self, wanted):
        if wanted not in self.known:
            out = self.base[wanted[0]]
            for name in wanted[1:]:
                out = out & self.base[name]
            self.known[wanted] = out
        return self.known[wanted]


def kv_states(k_rows, v_rows, first, count, after):
    rows = k_rows.shape[0]

    def kernel(ins, outs):
        for h in range(count):
            cols = head_cols(first + h)
            ka = silu(ins[0][:, cols])
            outs[1][:, head_cols(h)] = ka
            outs[0][h] = lax.dot_general(
                ka, ins[1][:, cols], (((0,), (0,)), ((), ())), preferred_element_type=F32
            ).astype(BF16)

    outs = [states_of(count, DH), jax.ShapeDtypeStruct((rows, count * DH), BF16)]
    return call(kernel, "kv_states", [k_rows, v_rows], outs, after, EARLY)


def local_scores(q_rows, ka, ka_first, first, count, after):
    rows = q_rows.shape[0]

    def kernel(ins, outs):
        q_ref, ka_ref = ins
        causal = lax.broadcasted_iota(jnp.int32, (rows, rows), 0) >= lax.broadcasted_iota(
            jnp.int32, (rows, rows), 1
        )
        for h in range(count):
            qa = silu(q_ref[:, head_cols(first + h)])
            scores = lax.dot_general(
                qa, ka_ref[:, head_cols(ka_first + h)], (((1,), (1,)), ((), ())),
                preferred_element_type=F32,
            )
            at = h * (rows + DH)
            outs[0][:, at : at + rows] = jnp.where(causal, scores, 0.0).astype(BF16)
            outs[0][:, at + rows : at + rows + DH] = qa

    out = jax.ShapeDtypeStruct((rows, count * (rows + DH)), BF16)
    return call(
        kernel, "local_scores", [q_rows, ka], [out], after
    )[0]


def attend_head(both_ref, v, state, h, rows):
    at = h * (rows + DH)
    right = jnp.concatenate([v, state.astype(BF16)], axis=0)
    return jnp.dot(
        both_ref[:, at : at + rows + DH], right, preferred_element_type=F32
    ).astype(BF16)


def attend(both, v_rows, first, terms, after):
    rows = both.shape[0]
    count = both.shape[1] // (rows + DH)

    def kernel(ins, outs):
        both_ref, v_ref, refs = ins[0], ins[1], ins[2:]
        held = Held()
        squares = None
        for h in range(count):
            state = term_sum(refs, terms, held, h)
            attn = attend_head(both_ref, v_ref[:, head_cols(first + h)], state, h, rows)
            outs[0][:, head_cols(h)] = attn
            wide = attn.astype(F32)
            squares = wide * wide if squares is None else squares + wide * wide
        outs[1][...] = squares

    outs = [
        jax.ShapeDtypeStruct((rows, count * DH), BF16),
        jax.ShapeDtypeStruct((rows, DH), F32),
    ]
    return call(kernel, "attend", [both, v_rows, *(t[0] for t in terms)], outs, after)


def last_attend(both, v_rows, first, terms, attns, squares, gain):
    rows, width = v_rows.shape
    count = both.shape[1] // (rows + DH)
    n_terms, n = len(terms), len(attns)
    starts = [0]
    for a in attns:
        starts.append(starts[-1] + a.shape[1])

    def kernel(*refs):
        both_ref, v_ref = refs[:2]
        term_refs = refs[2 : 2 + n_terms]
        attn_refs = refs[2 + n_terms : 2 + n_terms + n]
        sq_refs = refs[2 + n_terms + n : 2 + n_terms + 2 * n]
        gain_ref, out_hbm, done_ref, sem = refs[2 + n_terms + 2 * n :]
        held = Held()
        squares = None
        last = []
        for h in range(count):
            state = term_sum(term_refs, terms, held, h)
            attn = attend_head(both_ref, v_ref[:, head_cols(first + h)], state, h, rows)
            last.append(attn)
            wide = attn.astype(F32)
            squares = wide * wide if squares is None else squares + wide * wide
        for ref in sq_refs:
            squares = squares + ref[...]
        mean_sq = jnp.sum(squares, axis=1, keepdims=True) / width
        scale = jnp.broadcast_to(lax.rsqrt(mean_sq + 1e-06), (rows, DH))
        copies = []

        def send(start, wide):
            part = pl.ds(start, wide)
            copy = pltpu.make_async_copy(
                done_ref.at[:, part], out_hbm.at[0, :, part], sem.at[len(copies)]
            )
            copy.start()
            copies.append(copy)

        for i, start in enumerate(starts):
            wide = count * DH if i == n else attn_refs[i].shape[1]
            half = wide // DH // 2
            for h in range(wide // DH):
                if i == n and h == half:
                    send(start, half * DH)
                cols = slice(start + h * DH, start + (h + 1) * DH)
                attn = last[h] if i == n else attn_refs[i][:, head_cols(h)]
                done_ref[:, cols] = (attn.astype(F32) * scale * gain_ref[:, cols]).astype(BF16)
            if i == n:
                send(start + half * DH, wide - half * DH)
            else:
                send(start, wide)
        for copy in copies:
            copy.wait()

    operands = [both, v_rows, *(t[0] for t in terms), *attns, *squares, gain.reshape(1, width)]
    return pl.pallas_call(
        kernel,
        in_specs=[VMEM] * len(operands),
        out_specs=pl.BlockSpec(memory_space=pltpu.HBM),
        out_shape=jax.ShapeDtypeStruct((1, rows, width), BF16),
        scratch_shapes=[pltpu.VMEM((rows, width), BF16), pltpu.SemaphoreType.DMA((n + 2,))],
        compiler_params=pltpu.CompilerParams(vmem_limit_bytes=VMEM_LIMIT),
        cost_estimate=pl.CostEstimate(flops=COST, bytes_accessed=1, transcendentals=0),
        name="last_attend",
    )(*operands)


def total(*terms):
    out = terms[0].astype(F32)
    for term in terms[1:]:
        out = out + term.astype(F32)
    return out


def both_ways(pairs):
    return pairs + [(b, a) for a, b in pairs]


def before_ctx(n_ctx, own):
    odd = lax.axis_index("ctx") % 2 == 1
    before = jnp.zeros(own.shape, F32)
    if n_ctx % 2:
        for s in range(1, n_ctx):
            before = total(before, lax.ppermute(own, "ctx", [(i, i + s) for i in range(n_ctx - s)]))
        return before.astype(BF16)
    other = lax.ppermute(own, "ctx", both_ways([(i, i + 1) for i in range(0, n_ctx, 2)]))
    couple = total(own, other).astype(BF16)
    for s in range(2, n_ctx, 2):
        before = total(before, lax.ppermute(couple, "ctx", [(i, i + s) for i in range(n_ctx - s)]))
    return (before + jnp.where(odd, other.astype(F32), 0.0)).astype(BF16)


def whole_chain(n_head, own, early):
    upto = total(early, own)
    early = early.astype(F32)
    left = lax.axis_index("head") < n_head // 2
    if n_head == 1:
        return early.astype(BF16)
    if n_head % 2:
        lower = higher = jnp.zeros_like(own)
        for _ in range(n_head - 1):
            lower = lax.ppermute(
                total(lower, upto).astype(BF16), "head", [(i, i + 1) for i in range(n_head - 1)]
            )
            higher = lax.ppermute(
                total(higher, early).astype(BF16), "head", [(i + 1, i) for i in range(n_head - 1)]
            )
        return total(early, lower, higher).astype(BF16)
    mid = n_head // 2
    mine, mirror = jnp.where(left, upto, early), jnp.where(left, early, upto)
    inward = jnp.zeros_like(own)
    for t in range(mid - 1):
        inward = inward + lax.ppermute(
            total(inward, mine).astype(BF16), "head", [(t, t + 1), (n_head - 1 - t, n_head - 2 - t)]
        )
    outward = lax.ppermute(total(inward, mine).astype(BF16), "head", both_ways([(mid - 1, mid)]))
    for t in range(mid - 1, 0, -1):
        outward = outward + lax.ppermute(
            total(outward, mirror).astype(BF16), "head", [(t, t - 1), (n_head - 1 - t, n_head - t)]
        )
    return total(early, inward, outward).astype(BF16)


SKEW = 3
LATE = 2


def also(terms, *wanted):
    return [(array, first, (*had, *wanted)) for array, first, had in terms]


class Scan:
    def __init__(self, n, size):
        self.n, self.size = n, size
        self.own, self.other, self.x, self.a, self.b = {}, {}, {}, {}, {}
        self.late, self.late_other, self.whole = {}, {}, {}
        self.couples = both_ways([(0, 1), (2, 3)])
        self.across = both_ways([(0, 2), (1, 3)])
        at = lambda z, c: 4 * z + c
        self.swap = both_ways(
            [(at(1, c), at(2, c)) for c in range(4)]
            + [(at(z, c), at(z, c + 1)) for z in (0, 3) for c in (0, 2)]
        )

    def begin(self, first, own):
        if first < LATE:
            self.own[first] = (own, 0)
            return
        other = lax.ppermute(own, "ctx", self.couples)
        for i in range(own.shape[0] // self.size):
            self.own[first + i] = (own, i * self.size)
            self.other[first + i] = (other, i * self.size)

    def cross(self, c, after):
        terms = [(*self.own[c], ()), (*self.other[c], ())]
        send = combine("cross_sum", self.size, [terms], after, EARLY if c == LATE else COST)
        self.x[c] = (lax.ppermute(send, "ctx", self.across), 0)
        return [send]

    def early(self, c):
        return [(*self.other[c], ("odd",)), (*self.x[c], ("later",))]

    def mine(self, c):
        if c < LATE:
            return [(*self.own[c], ())]
        return [*self.early(c), (*self.own[c], ("left",))]

    def mirror(self, c):
        if c < LATE:
            return [(*self.own[c], ())]
        return [*self.early(c), (*self.own[c], ("right",))]

    def side(self, t, after):
        inwards, outwards = t < self.n, t >= SKEW
        c = t - SKEW
        terms = []
        if inwards:
            terms += also(self.mine(t), *(("outer",) if outwards else ()))
        if outwards:
            terms += also([*self.mirror(c), (*self.b[c], ())], *(("inner",) if inwards else ()))
        send = combine("side_sum", self.size, [terms], after, EARLY if t == 1 else COST)
        self.a[t] = (lax.ppermute(send, "head", both_ways([(0, 1), (3, 2)])), 0)
        return [send]

    def middle(self, t, after):
        send = combine("middle_sum", self.size, [[*self.mine(t), (*self.a[t], ())]], after)
        self.b[t] = (lax.ppermute(send, ("head", "ctx"), self.swap), 0)
        return [send]

    def lower(self, c):
        return [
            (*self.a[c], ("left", "inner")),
            (*self.b[c], ("right", "inner")),
            (*self.a[c + SKEW], ("right", "outer")),
        ]

    def higher(self, c):
        return [
            (*self.b[c], ("left", "inner")),
            (*self.a[c + SKEW], ("left", "outer")),
            (*self.a[c], ("right", "inner")),
        ]

    def late_cross(self, c, after):
        terms = [*self.lower(c), (*self.own[c], ()), *self.higher(c)]
        send = combine("late_sum", self.size, [terms], after, EARLY)
        self.whole[c] = (send, 0)
        self.late[c] = (lax.ppermute(send, "ctx", self.across), 0)
        return [send]

    def late_swap(self, c, after):
        terms = [(*self.late[c], ("later",)), (*self.whole[c], ("even",))]
        send = combine("late_swap", self.size, [terms], after, EARLY)
        self.late_other[c] = (lax.ppermute(send, "ctx", self.couples), 0)
        return [send]

    def state(self, c):
        if c < LATE:
            return [*self.lower(c), (*self.late[c], ("later",)), (*self.late_other[c], ())]
        return [
            *self.early(c),
            (*self.a[c], ("inner",)),
            (*self.b[c], ("inner",)),
            (*self.a[c + SKEW], ("outer",)),
        ]


def body(n_head, n_ctx, queries, keys, values, gain):
    rows, width = queries.shape[1], queries.shape[2]
    q_rows = queries.reshape(rows, width)
    k_rows = keys.reshape(rows, width)
    v_rows = values.reshape(rows, width)
    heads = width // DH
    if n_head != 4 or n_ctx != 4 or heads % 16:
        own, ka = kv_states(k_rows, v_rows, 0, heads, [])
        state = whole_chain(n_head, own, before_ctx(n_ctx, own))
        both = local_scores(q_rows, ka, 0, 0, heads, [])
        return last_attend(both, v_rows, 0, [(state, 0, ())], [], [], gain)

    n = 8
    size = heads // n
    both, attns, squares, ka = {}, {}, {}, {}
    scan = Scan(n, size)

    def kv(first, count, after, cut=False):
        at = first * size
        k, v = k_rows, v_rows
        if cut:
            cols = slice(at * DH, (at + count * size) * DH)
            k, v, at = k[:, cols], v[:, cols], 0
        own, active = kv_states(k, v, at, count * size, after)
        scan.begin(first, own)
        for i in range(count):
            ka[first + i] = (active, i * size)
        return [own]

    def scores(c, after):
        both[c] = local_scores(q_rows, *ka[c], c * size, size, after)
        return [both[c]]

    def attention(c, after):
        attns[c], squares[c] = attend(both[c], v_rows, c * size, scan.state(c), after)
        return [squares[c]]

    fill = {
        1: [0], 2: [1], 3: [2], 4: [3], 5: [4], 6: [5], 7: [6], 8: [7],
    }
    clock = kv(2, 1, [], cut=True)
    clock = kv(0, 1, clock, cut=True)
    for t in range(n + SKEW):
        clock = scan.side(t, clock)
        if t == 0:
            clock = kv(1, 1, clock, cut=True)
        if t == 1:
            clock = scan.cross(2, clock)
            clock = kv(3, 1, clock)
            clock = kv(4, 4, clock)
        if t == n + 1:
            clock = scan.late_swap(0, clock)
        if t == n + 2:
            clock = scan.late_swap(1, clock)
        for c in fill.get(t, []):
            clock = scores(c, clock)
        if t > n:
            clock = attention(t - n - 1 + LATE, clock)
        if 0 <= t - 1 < n:
            clock = scan.middle(t - 1, clock)
        if LATE < t + 2 < n:
            clock = scan.cross(t + 2, clock)
        if 0 <= t + 2 - n < LATE:
            clock = scan.late_cross(t + 2 - n, clock)
    for c in [*range(LATE, n - 1), *range(LATE)]:
        if c not in attns:
            clock = attention(c, clock)
    return last_attend(
        both[n - 1], v_rows, (n - 1) * size, scan.state(n - 1),
        [attns[c] for c in range(n - 1)], [squares[c] for c in range(n - 1)], gain,
    )


def solution(mesh):
    n_head, n_ctx = mesh.shape["head"], mesh.shape["ctx"]
    return jax.shard_map(
        functools.partial(body, n_head, n_ctx),
        mesh=mesh,
        in_specs=(
            P(("rep", "ctx"), "head", None),
            P(("rep", "ctx"), "head", None),
            P(("rep", "ctx"), "head", None),
            P(),
        ),
        out_specs=P(("rep", "ctx"), "head", None),
        check_vma=False,
    )
```
